512 devices in a mesh: pair: 32 (over y, z_lo), row: 16 (over z_hi, x, core).
Axes of the slice: x: 4, y: 4, z: 16 (z_hi: 2, z_lo: 8; z = z_hi * 8 + z_lo), core: 2. Of those that a mesh axis runs over, the one named last changes fastest.
Arguments:
- factor: float32 [8192, 16384], P('row', 'pair'), may hold values from -6 to 6
- plan: int32 [2, 512], replicated, may hold values from 0 to 511, each once within a row
Outputs:
- rotated: float32 [8192, 16384], P('row', 'pair')
The draws below stay inside these ranges and needn't reach their ends.
Inputs may be any that keep to these rules, and one draw needn't show every extreme that they name: Each row of plan names every number of 0 to 511 once.
All inputs are finite; a program needn't handle non-finite values.
Results may differ from the reference program's by a relative error of at most 0.0001.
Values sent between devices are 32-bit elements; how exact they have to be, the bound alone decides.
A program may use at most 64 MiB of HBM per device.

```python
import jax
import jax.numpy as jnp
from jax import lax

BLK = 256
ROUNDS = 2
NS_STEPS = 3
PAIR_COLS = 512
ROWS = 8192
NCOLS = 16384


def block_scale(key, dims, split, smallest, high):
    factor_of = 1.0
    for dim, parts in split:
        draws = jax.random.uniform(jax.random.fold_in(jax.random.fold_in(key, 6), dim), (parts,), jnp.float32, smallest / len(split), high / len(split))
        factor_of = factor_of * jnp.repeat(jnp.exp(draws), dims[dim] // parts).reshape((-1,) + (1,) * (len(dims) - 1 - dim))
    return factor_of


def noise(key, shape, scale, most, cuts=(), held_as=jnp.bfloat16):
    factor_of = block_scale(key, shape, cuts, -0.22, 0.18) if cuts else 1.0
    values = jax.random.normal(key, shape, jnp.float32) * scale * factor_of
    return jnp.minimum(jnp.maximum(values, -most), most).astype(held_as)


def setup_inputs(seed: int = 0) -> dict:
    splits = jax.random.split(jax.random.key(seed), 3)
    return {
        "factor": noise(splits[0], (ROWS, NCOLS), 1.0, 6.0, ((0, 16), (1, 32)), jnp.float32),
        "plan": jax.vmap(lambda own: jax.random.permutation(own, PAIR_COLS))(jax.random.split(splits[1], ROUNDS)).reshape((ROUNDS, PAIR_COLS)).astype(jnp.int32),
    }


eps_value = 1e-06

def reference(factor, plan):
    total_rows = factor.shape[0]
    width = 2 * BLK
    npairs = factor.shape[1] // width
    blocks = factor.reshape(total_rows, npairs, width)
    index = jnp.arange(width)
    upper = index < BLK
    positive = upper[:, None] & jnp.logical_not(upper)[None, :]
    negative = jnp.logical_not(upper)[:, None] & upper[None, :]
    sign = jnp.where(positive, 1.0, jnp.where(negative, -1.0, 0.0)).astype(jnp.float32)
    identity = jnp.eye(width, dtype=jnp.float32)
    highest = lax.Precision.HIGHEST
    for rnd in range(ROUNDS):
        work = jnp.take(blocks, plan[rnd].astype(jnp.int32), axis=2)
        gram = jnp.einsum('rpi,rpj->pij', work, work, precision=highest)
        diag = jnp.diagonal(gram, axis1=1, axis2=2)
        inverse = 1.0 / jnp.sqrt(diag + eps_value)
        normed = gram * inverse[:, :, None] * inverse[:, None, :]
        total = lax.optimization_barrier(jnp.sum(jnp.where(positive[None], normed * normed, 0.0), axis=(1, 2)))
        scale = 1.0 / (1.0 + jnp.sqrt(total))
        iterate = identity[None] + sign[None] * normed * scale[:, None, None]
        for step in range(NS_STEPS):
            square = jnp.einsum('pki,pkj->pij', iterate, iterate, precision=highest)
            iterate = 1.5 * iterate - 0.5 * jnp.einsum('pik,pkj->pij', iterate, square, precision=highest)
        work = jnp.einsum('rpi,pij->rpj', work, iterate, precision=highest)
        second = jnp.roll(work[:, :, BLK:], 1, axis=1)
        blocks = jnp.concatenate([work[:, :, :BLK], second], axis=2)
    return blocks.reshape(total_rows, npairs * width)
```

```python
import functools

import jax
import jax.numpy as jnp
from jax import lax
from jax.experimental import pallas as pl
from jax.experimental.pallas import tpu as pltpu
from jax.sharding import PartitionSpec as P

BLK = 256
ROUNDS = 2
WIDTH = 2 * BLK
LANES = 128
XCHIPS = 4
PIECES = 8
PIECE = BLK // PIECES
TALL = 2 * PIECE
PACKED = TALL + 8
CHUNKS = 4
MESH = pl.DeviceIdType.MESH

eps_value = 1e-06

f32 = jnp.float32
bf16 = jnp.bfloat16


def dot(left, right, dims=((1,), (0,))):
    return lax.dot_general(left, right, (dims, ((), ())), preferred_element_type=f32)


def halves(value):
    high = value.astype(bf16)
    return high, (value - high.astype(f32)).astype(bf16)


def product(left, right, dims=((1,), (0,))):
    (lh, ll), (rh, rl) = left, right
    return dot(lh, rh, dims) + (dot(lh, rl, dims) + dot(ll, rh, dims))


def polar_part(coupling, unit):
    parts = halves(coupling)
    a = product(parts, parts, ((1,), (1,)))
    ap = halves(a)
    a2 = product(ap, ap)
    e1 = 0.25 * product(halves(a2), ap) - 0.75 * a2
    e1p = halves(e1)
    sq = product(e1p, e1p)
    e2 = 0.25 * product(halves(sq), e1p) - 0.75 * sq
    off = 0.25 * product(ap, e1p) - 0.5 * (a + e1)
    return unit + (off - 0.5 * (e2 + product(halves(off), halves(e2))))


def kernel(
    plan_ref, factor_ref, out_ref,
    hot, wh, wl, fh, fl, xh, xl, part, from_core, half_sum, from_x, own_sum, from_z, grid_c, ship, land,
    core_send, core_recv, x_send, x_recv, z_send, z_recv, gx_send, gx_recv, gc_send, gc_recv, s_send, s_recv,
):
    pairs = lax.axis_size("pair")
    p, r = lax.axis_index("pair"), lax.axis_index("row")
    core, x, zh = r % 2, (r // 2) % XCHIPS, r // (2 * XCHIPS)
    sibling = (p, r + 1 - 2 * core)
    across = (p, (r + 2 * XCHIPS) % (4 * XCHIPS))
    after, before = ((p + 1) % pairs, r), ((p + pairs - 1) % pairs, r)

    def x_peer(by):
        return (p, zh * (2 * XCHIPS) + ((x + by) % XCHIPS) * 2 + core)

    barrier = pltpu.get_barrier_semaphore()
    for peer in (sibling, x_peer(1), x_peer(2), x_peer(3), across, before):
        pl.semaphore_signal(barrier, inc=1, device_id=peer, device_id_type=MESH)

    rows = out_ref.shape[0]
    step = rows // CHUNKS
    row_ids = lax.broadcasted_iota(jnp.int32, (BLK, BLK), 0)
    col_ids = lax.broadcasted_iota(jnp.int32, (BLK, BLK), 1)
    on_diagonal = row_ids == col_ids

    def remote(src, dst, send, recv, to):
        return pltpu.make_async_remote_copy(
            src_ref=src, dst_ref=dst, send_sem=send, recv_sem=recv, device_id=to, device_id_type=MESH
        )

    started = []

    def reorder(span, high, low):
        moved_h = dot(high, hot[...])
        moved_l = dot(low, hot[...])
        wh[span, :] = moved_h.astype(bf16)
        wl[span, :] = moved_l.astype(bf16)
        moved = moved_h + moved_l
        return jnp.sum(moved * moved, axis=0, keepdims=True)

    def coupling_of(span):
        first = (wh[span, :BLK], wl[span, :BLK])
        second = (wh[span, BLK:], wl[span, BLK:])
        return product(first, second, ((0,), (0,)))

    for rnd in range(ROUNDS):
        order = plan_ref[rnd : rnd + 1, :]
        hot[...] = jnp.where(
            lax.broadcasted_iota(jnp.int32, (WIDTH, WIDTH), 0) == order, 1.0, 0.0
        ).astype(bf16)

        squares = jnp.zeros((1, WIDTH), f32)
        cross = jnp.zeros((BLK, BLK), f32)
        for chunk in range(CHUNKS):
            span = slice(chunk * step, (chunk + 1) * step)
            if rnd == 0:
                high, low = halves(factor_ref[span, :])
            else:
                remote(
                    ship.at[rnd - 1, span, :], land.at[span, :],
                    s_send.at[rnd - 1, chunk], s_recv.at[rnd - 1, chunk], after,
                ).wait_recv()
                sh, sl = halves(land[span, :])
                high = jnp.concatenate([fh[span, :], sh], axis=1)
                low = jnp.concatenate([fl[span, :], sl], axis=1)
            squares += reorder(span, high, low)
            cross += coupling_of(span)

        tile = jnp.concatenate(
            [squares[:, i * LANES : (i + 1) * LANES] for i in range(4)] + [jnp.zeros((4, LANES), f32)], axis=0
        )
        for piece in range(PIECES):
            for side in range(2):
                part[rnd, piece, side * PIECE : (side + 1) * PIECE, :] = cross[
                    piece * PIECE : (piece + 1) * PIECE, side * LANES : (side + 1) * LANES
                ]
            part[rnd, piece, TALL:, :] = tile

        if rnd == 0:
            pl.semaphore_wait(barrier, 6)

        swap = remote(
            part.at[rnd, pl.ds((1 - core) * XCHIPS, XCHIPS)], from_core.at[rnd],
            core_send.at[rnd], core_recv.at[rnd], sibling,
        )
        swap.start()
        started.append(swap)
        swap.wait_recv()
        for other in range(XCHIPS):
            half_sum[rnd, other] = part[rnd, core * XCHIPS + other] + from_core[rnd, other]

        spread = []
        for by in (2, 1, 3):
            copy = remote(
                half_sum.at[rnd, (x + by) % XCHIPS], from_x.at[rnd, by - 1],
                x_send.at[rnd, by - 1], x_recv.at[rnd, by - 1], x_peer(by),
            )
            copy.start()
            spread.append(copy)
        started += spread
        for copy in spread:
            copy.wait_recv()
        own_sum[rnd] = (half_sum[rnd, x] + from_x[rnd, 0]) + (from_x[rnd, 1] + from_x[rnd, 2])

        swap = remote(own_sum.at[rnd], from_z.at[rnd], z_send.at[rnd], z_recv.at[rnd], across)
        swap.start()
        started.append(swap)
        swap.wait_recv()
        total_piece = own_sum[rnd] + from_z[rnd]
        mine = core * XCHIPS + x
        grid_c[rnd, mine] = total_piece[:TALL, :]

        spread = []
        for by in (2, 1, 3):
            copy = remote(
                grid_c.at[rnd, mine], grid_c.at[rnd, mine],
                gx_send.at[rnd, by - 1], gx_recv.at[rnd, by - 1], x_peer(by),
            )
            copy.start()
            spread.append(copy)
        started += spread
        passed = []
        for by in (0, 1, 3, 2):
            slot = core * XCHIPS + (x + XCHIPS - by) % XCHIPS
            if by:
                remote(
                    grid_c.at[rnd, mine], grid_c.at[rnd, slot],
                    gx_send.at[rnd, by - 1], gx_recv.at[rnd, by - 1], x_peer(by),
                ).wait_recv()
            copy = remote(
                grid_c.at[rnd, slot], grid_c.at[rnd, slot], gc_send.at[rnd, by], gc_recv.at[rnd, by], sibling
            )
            copy.start()
            passed.append(copy)
        started += passed
        for copy in passed:
            copy.wait_recv()

        gram_c = jnp.concatenate(
            [
                jnp.concatenate([grid_c[rnd, piece, :PIECE, :], grid_c[rnd, piece, PIECE:, :]], axis=1)
                for piece in range(PIECES)
            ],
            axis=0,
        )
        inverse = 1.0 / jnp.sqrt(total_piece[TALL:, :] + eps_value)
        inv_top = jnp.concatenate([inverse[0:1, :], inverse[1:2, :]], axis=1)
        inv_side = jnp.concatenate([inverse[2:3, :], inverse[3:4, :]], axis=1)
        inv_rows = jnp.sum(jnp.where(on_diagonal, inv_top, 0.0), axis=1, keepdims=True)
        normed = gram_c * inv_rows * inv_side
        total = jnp.sum(jnp.sum(normed * normed, axis=0, keepdims=True), axis=1, keepdims=True)
        coupling = normed * (1.0 / (1.0 + jnp.sqrt(total)))

        unit = jnp.where(on_diagonal, 1.0, 0.0)
        top = polar_part(coupling, unit)
        bottom_parts = halves(polar_part(coupling.T, unit))
        turn = product(halves(coupling), bottom_parts)
        xh[:BLK, :BLK], xl[:BLK, :BLK] = halves(top)
        xh[BLK:, BLK:], xl[BLK:, BLK:] = bottom_parts
        xh[:BLK, BLK:], xl[:BLK, BLK:] = halves(turn)
        xh[BLK:, :BLK], xl[BLK:, :BLK] = halves(-turn.T)

        last = rnd == ROUNDS - 1
        for chunk in range(CHUNKS):
            span = slice(chunk * step, (chunk + 1) * step)
            ship[rnd, span, :] = product((wh[span, :], wl[span, :]), (xh[:, BLK:], xl[:, BLK:]))
            copy = remote(
                ship.at[rnd, span, :], out_ref.at[span, pl.ds(BLK, BLK)] if last else land.at[span, :],
                s_send.at[rnd, chunk], s_recv.at[rnd, chunk], after,
            )
            copy.start()
            started.append(copy)
        for chunk in range(CHUNKS):
            span = slice(chunk * step, (chunk + 1) * step)
            kept = product((wh[span, :], wl[span, :]), (xh[:, :BLK], xl[:, :BLK]))
            if last:
                out_ref[span, :BLK] = kept
            else:
                fh[span, :], fl[span, :] = halves(kept)

    for chunk in range(CHUNKS):
        started[-CHUNKS + chunk].wait_recv()
    for copy in started:
        copy.wait_send()


def shards(factor, plan):
    rows = factor.shape[0]
    dma = pltpu.SemaphoreType.DMA
    return pl.pallas_call(
        kernel,
        out_shape=jax.ShapeDtypeStruct((rows, WIDTH), f32),
        in_specs=[pl.BlockSpec(memory_space=pltpu.VMEM)] * 2,
        out_specs=pl.BlockSpec(memory_space=pltpu.VMEM),
        scratch_shapes=[
            pltpu.VMEM((WIDTH, WIDTH), bf16),
            pltpu.VMEM((rows, WIDTH), bf16),
            pltpu.VMEM((rows, WIDTH), bf16),
            pltpu.VMEM((rows, BLK), bf16),
            pltpu.VMEM((rows, BLK), bf16),
            pltpu.VMEM((WIDTH, WIDTH), bf16),
            pltpu.VMEM((WIDTH, WIDTH), bf16),
            pltpu.VMEM((ROUNDS, PIECES, PACKED, LANES), f32),
            pltpu.VMEM((ROUNDS, XCHIPS, PACKED, LANES), f32),
            pltpu.VMEM((ROUNDS, XCHIPS, PACKED, LANES), f32),
            pltpu.VMEM((ROUNDS, XCHIPS - 1, PACKED, LANES), f32),
            pltpu.VMEM((ROUNDS, PACKED, LANES), f32),
            pltpu.VMEM((ROUNDS, PACKED, LANES), f32),
            pltpu.VMEM((ROUNDS, PIECES, TALL, LANES), f32),
            pltpu.VMEM((ROUNDS, rows, BLK), f32),
            pltpu.VMEM((rows, BLK), f32),
            dma((ROUNDS,)), dma((ROUNDS,)),
            dma((ROUNDS, 3)), dma((ROUNDS, 3)),
            dma((ROUNDS,)), dma((ROUNDS,)),
            dma((ROUNDS, 3)), dma((ROUNDS, 3)),
            dma((ROUNDS, 4)), dma((ROUNDS, 4)),
            dma((ROUNDS, CHUNKS)), dma((ROUNDS, CHUNKS)),
        ],
        compiler_params=pltpu.CompilerParams(collective_id=0, has_side_effects=True),
    )(plan, factor)


def solution(mesh):
    placed = (P("row", "pair"), P())
    return jax.shard_map(
        shards, mesh=mesh, in_specs=placed, out_specs=P("row", "pair"), check_vma=False
    )
```

```python
import functools

import jax
import jax.numpy as jnp
from jax import lax
from jax.experimental import pallas as pl
from jax.experimental.pallas import tpu as pltpu
from jax.sharding import PartitionSpec as P

BLK = 256
ROUNDS = 2
WIDTH = 2 * BLK
LANES = 128
XCHIPS = 4
PIECES = 8
PIECE = BLK // PIECES
TALL = 2 * PIECE
PACKED = TALL + 8
EDGES = (0, 64, 192, 320, 448, 512)
SPANS = tuple(slice(low, high) for low, high in zip(EDGES, EDGES[1:]))
MESH = pl.DeviceIdType.MESH

eps_value = 1e-06

f32 = jnp.float32
bf16 = jnp.bfloat16


def dot(left, right, dims=((1,), (0,))):
    return lax.dot_general(left, right, (dims, ((), ())), preferred_element_type=f32)


def halves(value):
    high = value.astype(bf16)
    return high, (value - high.astype(f32)).astype(bf16)


def product(left, right, dims=((1,), (0,))):
    (lh, ll), (rh, rl) = left, right
    return dot(lh, rh, dims) + (dot(lh, rl, dims) + dot(ll, rh, dims))


def polar_part(coupling, unit):
    parts = halves(coupling)
    a = product(parts, parts, ((1,), (1,)))
    ap = halves(a)
    a2 = product(ap, ap)
    e1 = 0.25 * product(halves(a2), ap) - 0.75 * a2
    e1p = halves(e1)
    sq = product(e1p, e1p)
    e2 = 0.25 * product(halves(sq), e1p) - 0.75 * sq
    off = 0.25 * product(ap, e1p) - 0.5 * (a + e1)
    return unit + (off - 0.5 * (e2 + product(halves(off), halves(e2))))


def kernel(
    plan_ref, factor_ref, out_ref,
    hot, wh, wl, fh, fl, xh, xl, part, from_core, half_sum, from_x, own_sum, from_z, grid_c, ship, land,
    core_send, core_recv, x_send, x_recv, z_send, z_recv, gx_send, gx_recv, gc_send, gc_recv, s_send, s_recv, near_in, far_in,
):
    pairs = lax.axis_size("pair")
    p, r = lax.axis_index("pair"), lax.axis_index("row")
    core, x, zh = r % 2, (r // 2) % XCHIPS, r // (2 * XCHIPS)
    sibling = (p, r + 1 - 2 * core)
    across = (p, (r + 2 * XCHIPS) % (4 * XCHIPS))
    after, before = ((p + 1) % pairs, r), ((p + pairs - 1) % pairs, r)

    def x_peer(by):
        return (p, zh * (2 * XCHIPS) + ((x + by) % XCHIPS) * 2 + core)

    barrier = pltpu.get_barrier_semaphore()

    def enter(pair, row):
        pl.semaphore_signal(barrier, inc=1, device_id=(pair, row), device_id_type=MESH)

    for by in (1, 2, 3):
        enter(p, x_peer(by)[1] - core)
    enter(across[0], across[1] - core + 1)
    enter(before[0], before[1] - core + 1)

    @pl.when(core == 1)
    def _():
        enter(p, r - 1)

    def pass_on(count, told, teller):
        @pl.when(core == teller)
        def _():
            pl.semaphore_wait(barrier, count)
            pl.semaphore_signal(told, inc=1, device_id=sibling, device_id_type=MESH)

        @pl.when(core != teller)
        def _():
            pl.semaphore_wait(told, 1)

    row_ids = lax.broadcasted_iota(jnp.int32, (BLK, BLK), 0)
    col_ids = lax.broadcasted_iota(jnp.int32, (BLK, BLK), 1)
    on_diagonal = row_ids == col_ids

    def remote(src, dst, send, recv, to):
        return pltpu.make_async_remote_copy(
            src_ref=src, dst_ref=dst, send_sem=send, recv_sem=recv, device_id=to, device_id_type=MESH
        )

    started = []

    def reorder(span, high, low):
        moved_h = dot(high, hot[...])
        moved_l = dot(low, hot[...])
        wh[span, :] = moved_h.astype(bf16)
        wl[span, :] = moved_l.astype(bf16)
        moved = moved_h + moved_l
        return jnp.sum(moved * moved, axis=0, keepdims=True)

    def coupling_of(span):
        first = (wh[span, :BLK], wl[span, :BLK])
        second = (wh[span, BLK:], wl[span, BLK:])
        return product(first, second, ((0,), (0,)))

    for rnd in range(ROUNDS):
        order = plan_ref[rnd : rnd + 1, :]
        hot[...] = jnp.where(
            lax.broadcasted_iota(jnp.int32, (WIDTH, WIDTH), 0) == order, 1.0, 0.0
        ).astype(bf16)

        squares = jnp.zeros((1, WIDTH), f32)
        cross = jnp.zeros((BLK, BLK), f32)
        for chunk, span in enumerate(SPANS):
            if rnd == 0:
                high, low = halves(factor_ref[span, :])
            else:
                remote(
                    ship.at[rnd - 1, span, :], land.at[span, :],
                    s_send.at[rnd - 1, chunk], s_recv.at[rnd - 1, chunk], after,
                ).wait_recv()
                sh, sl = halves(land[span, :])
                high = jnp.concatenate([fh[span, :], sh], axis=1)
                low = jnp.concatenate([fl[span, :], sl], axis=1)
            squares += reorder(span, high, low)
            cross += coupling_of(span)

        tile = jnp.concatenate(
            [squares[:, i * LANES : (i + 1) * LANES] for i in range(4)] + [jnp.zeros((4, LANES), f32)], axis=0
        )
        for piece in range(PIECES):
            for side in range(2):
                part[rnd, piece, side * PIECE : (side + 1) * PIECE, :] = cross[
                    piece * PIECE : (piece + 1) * PIECE, side * LANES : (side + 1) * LANES
                ]
            part[rnd, piece, TALL:, :] = tile

        if rnd == 0:
            pass_on(7, near_in, 0)

        swap = remote(
            part.at[rnd, pl.ds((1 - core) * XCHIPS, XCHIPS)], from_core.at[rnd],
            core_send.at[rnd], core_recv.at[rnd], sibling,
        )
        swap.start()
        started.append(swap)
        swap.wait_recv()
        for other in range(XCHIPS):
            half_sum[rnd, other] = part[rnd, core * XCHIPS + other] + from_core[rnd, other]

        spread = []
        for by in (2, 1, 3):
            copy = remote(
                half_sum.at[rnd, (x + by) % XCHIPS], from_x.at[rnd, by - 1],
                x_send.at[rnd, by - 1], x_recv.at[rnd, by - 1], x_peer(by),
            )
            copy.start()
            spread.append(copy)
        started += spread
        for copy in spread:
            copy.wait_recv()
        own_sum[rnd] = (half_sum[rnd, x] + from_x[rnd, 0]) + (from_x[rnd, 1] + from_x[rnd, 2])

        if rnd == 0:
            pass_on(4, far_in, 1)
        swap = remote(own_sum.at[rnd], from_z.at[rnd], z_send.at[rnd], z_recv.at[rnd], across)
        swap.start()
        started.append(swap)
        swap.wait_recv()
        total_piece = own_sum[rnd] + from_z[rnd]
        mine = core * XCHIPS + x
        grid_c[rnd, mine] = total_piece[:TALL, :]

        spread = []
        for by in (2, 1, 3):
            copy = remote(
                grid_c.at[rnd, mine], grid_c.at[rnd, mine],
                gx_send.at[rnd, by - 1], gx_recv.at[rnd, by - 1], x_peer(by),
            )
            copy.start()
            spread.append(copy)
        started += spread
        passed = []
        for by in (0, 1, 3, 2):
            slot = core * XCHIPS + (x + XCHIPS - by) % XCHIPS
            if by:
                remote(
                    grid_c.at[rnd, mine], grid_c.at[rnd, slot],
                    gx_send.at[rnd, by - 1], gx_recv.at[rnd, by - 1], x_peer(by),
                ).wait_recv()
            copy = remote(
                grid_c.at[rnd, slot], grid_c.at[rnd, slot], gc_send.at[rnd, by], gc_recv.at[rnd, by], sibling
            )
            copy.start()
            passed.append(copy)
        started += passed
        for copy in passed:
            copy.wait_recv()

        gram_c = jnp.concatenate(
            [
                jnp.concatenate([grid_c[rnd, piece, :PIECE, :], grid_c[rnd, piece, PIECE:, :]], axis=1)
                for piece in range(PIECES)
            ],
            axis=0,
        )
        inverse = 1.0 / jnp.sqrt(total_piece[TALL:, :] + eps_value)
        inv_top = jnp.concatenate([inverse[0:1, :], inverse[1:2, :]], axis=1)
        inv_side = jnp.concatenate([inverse[2:3, :], inverse[3:4, :]], axis=1)
        inv_rows = jnp.sum(jnp.where(on_diagonal, inv_top, 0.0), axis=1, keepdims=True)
        normed = gram_c * inv_rows * inv_side
        total = jnp.sum(jnp.sum(normed * normed, axis=0, keepdims=True), axis=1, keepdims=True)
        coupling = normed * (1.0 / (1.0 + jnp.sqrt(total)))

        unit = jnp.where(on_diagonal, 1.0, 0.0)
        corner = halves(polar_part(coupling.T, unit))
        turn = product(halves(coupling), corner)
        xh[BLK:, BLK:], xl[BLK:, BLK:] = corner
        xh[:BLK, BLK:], xl[:BLK, BLK:] = halves(turn)

        last = rnd == ROUNDS - 1
        for chunk, span in enumerate(SPANS):
            ship[rnd, span, :] = product((wh[span, :], wl[span, :]), (xh[:, BLK:], xl[:, BLK:]))
            copy = remote(
                ship.at[rnd, span, :], out_ref.at[span, pl.ds(BLK, BLK)] if last else land.at[span, :],
                s_send.at[rnd, chunk], s_recv.at[rnd, chunk], after,
            )
            copy.start()
            started.append(copy)
        xh[:BLK, :BLK], xl[:BLK, :BLK] = halves(polar_part(coupling, unit))
        xh[BLK:, :BLK], xl[BLK:, :BLK] = halves(-turn.T)
        for span in SPANS:
            kept = product((wh[span, :], wl[span, :]), (xh[:, :BLK], xl[:, :BLK]))
            if last:
                out_ref[span, :BLK] = kept
            else:
                fh[span, :], fl[span, :] = halves(kept)

    for copy in started[-len(SPANS):]:
        copy.wait_recv()
    for copy in started:
        copy.wait_send()


def shards(factor, plan):
    rows = factor.shape[0]
    dma = pltpu.SemaphoreType.DMA
    return pl.pallas_call(
        kernel,
        out_shape=jax.ShapeDtypeStruct((rows, WIDTH), f32),
        in_specs=[pl.BlockSpec(memory_space=pltpu.VMEM)] * 2,
        out_specs=pl.BlockSpec(memory_space=pltpu.VMEM),
        scratch_shapes=[
            pltpu.VMEM((WIDTH, WIDTH), bf16),
            pltpu.VMEM((rows, WIDTH), bf16),
            pltpu.VMEM((rows, WIDTH), bf16),
            pltpu.VMEM((rows, BLK), bf16),
            pltpu.VMEM((rows, BLK), bf16),
            pltpu.VMEM((WIDTH, WIDTH), bf16),
            pltpu.VMEM((WIDTH, WIDTH), bf16),
            pltpu.VMEM((ROUNDS, PIECES, PACKED, LANES), f32),
            pltpu.VMEM((ROUNDS, XCHIPS, PACKED, LANES), f32),
            pltpu.VMEM((ROUNDS, XCHIPS, PACKED, LANES), f32),
            pltpu.VMEM((ROUNDS, XCHIPS - 1, PACKED, LANES), f32),
            pltpu.VMEM((ROUNDS, PACKED, LANES), f32),
            pltpu.VMEM((ROUNDS, PACKED, LANES), f32),
            pltpu.VMEM((ROUNDS, PIECES, TALL, LANES), f32),
            pltpu.VMEM((ROUNDS, rows, BLK), f32),
            pltpu.VMEM((rows, BLK), f32),
            dma((ROUNDS,)), dma((ROUNDS,)),
            dma((ROUNDS, 3)), dma((ROUNDS, 3)),
            dma((ROUNDS,)), dma((ROUNDS,)),
            dma((ROUNDS, 3)), dma((ROUNDS, 3)),
            dma((ROUNDS, 4)), dma((ROUNDS, 4)),
            dma((ROUNDS, len(SPANS))), dma((ROUNDS, len(SPANS))),
            pltpu.SemaphoreType.REGULAR, pltpu.SemaphoreType.REGULAR,
        ],
        compiler_params=pltpu.CompilerParams(
            collective_id=0, has_side_effects=True, vmem_limit_bytes=20 << 20
        ),
    )(plan, factor)


def solution(mesh):
    placed = (P("row", "pair"), P())
    return jax.shard_map(
        shards, mesh=mesh, in_specs=placed, out_specs=P("row", "pair"), check_vma=False
    )
```

```python
import functools

import jax
import jax.numpy as jnp
from jax import lax
from jax.experimental import pallas as pl
from jax.experimental.pallas import tpu as pltpu
from jax.sharding import PartitionSpec as P

BLK = 256
ROUNDS = 2
WIDTH = 2 * BLK
LANES = 128
XCHIPS = 4
PIECES = 8
PIECE = BLK // PIECES
TALL = 2 * PIECE
PACKED = TALL + 8
EARLY = 256
STEP = 64
AHEAD = 3


def spans(low, high, by):
    return tuple(slice(at, min(at + by, high)) for at in range(low, high, by))


FIRST = spans(0, EARLY, STEP)
MESH = pl.DeviceIdType.MESH

eps_value = 1e-06

f32 = jnp.float32
bf16 = jnp.bfloat16


def dot(left, right, dims=((1,), (0,))):
    return lax.dot_general(left, right, (dims, ((), ())), preferred_element_type=f32)


def halves(value):
    high = value.astype(bf16)
    return high, (value - high.astype(f32)).astype(bf16)


def product(left, right, dims=((1,), (0,))):
    (lh, ll), (rh, rl) = left, right
    return dot(lh, rh, dims) + (dot(lh, rl, dims) + dot(ll, rh, dims))


def polar_part(coupling, unit):
    parts = halves(coupling)
    a = product(parts, parts, ((1,), (1,)))
    ap = halves(a)
    a2 = product(ap, ap)
    e1 = 0.25 * product(halves(a2), ap) - 0.75 * a2
    e1p = halves(e1)
    sq = product(e1p, e1p)
    e2 = 0.25 * product(halves(sq), e1p) - 0.75 * sq
    off = 0.25 * product(ap, e1p) - 0.5 * (a + e1)
    return unit + (off - 0.5 * (e2 + product(halves(off), halves(e2))))


def kernel(
    plan_ref, factor_ref, out_ref,
    hot, wh, wl, fh, fl, xh, xl, part, from_core, half_sum, from_x, own_sum, from_z, sum_c, grid_c, ship, land,
    mid, raw, uh, ul, from_before, grid_b,
    core_send, core_recv, x_send, x_recv, z_send, z_recv, gx_send, gx_recv, gc_send, gc_recv, s_send, s_recv,
    r_send, r_recv, b_send, b_recv, bx_send, bx_recv, bc_send, bc_recv, near_in, far_in,
):
    pairs = lax.axis_size("pair")
    p, r = lax.axis_index("pair"), lax.axis_index("row")
    core, x, zh = r % 2, (r // 2) % XCHIPS, r // (2 * XCHIPS)
    sibling = (p, r + 1 - 2 * core)
    across = (p, (r + 2 * XCHIPS) % (4 * XCHIPS))
    after, before = ((p + 1) % pairs, r), ((p + pairs - 1) % pairs, r)
    mine = core * XCHIPS + x

    def x_peer(by):
        return (p, zh * (2 * XCHIPS) + ((x + by) % XCHIPS) * 2 + core)

    barrier = pltpu.get_barrier_semaphore()

    def enter(pair, row):
        pl.semaphore_signal(barrier, inc=1, device_id=(pair, row), device_id_type=MESH)

    for by in (1, 2, 3):
        enter(p, x_peer(by)[1] - core)
    enter(across[0], across[1] - core + 1)
    enter(before[0], before[1] - core + 1)

    @pl.when(core == 1)
    def _():
        enter(p, r - 1)

    def pass_on(count, told, teller):
        @pl.when(core == teller)
        def _():
            pl.semaphore_wait(barrier, count)
            pl.semaphore_signal(told, inc=1, device_id=sibling, device_id_type=MESH)

        @pl.when(core != teller)
        def _():
            pl.semaphore_wait(told, 1)

    row_ids = lax.broadcasted_iota(jnp.int32, (BLK, BLK), 0)
    col_ids = lax.broadcasted_iota(jnp.int32, (BLK, BLK), 1)
    on_diagonal = row_ids == col_ids
    rows = out_ref.shape[0]
    late = spans(EARLY, rows, STEP)

    def remote(src, dst, send, recv, to):
        return pltpu.make_async_remote_copy(
            src_ref=src, dst_ref=dst, send_sem=send, recv_sem=recv, device_id=to, device_id_type=MESH
        )

    started = []

    def go(src, dst, send, recv, to):
        copy = remote(src, dst, send, recv, to)
        copy.start()
        started.append(copy)
        return copy

    def reorder(high, low):
        return dot(high, hot[...]), dot(low, hot[...])

    def gather_start(rnd, src, pieces, sends, recvs):
        for by in (2, 1, 3):
            go(src, pieces.at[rnd, mine], sends.at[rnd, by - 1], recvs.at[rnd, by - 1], x_peer(by))

    def gather_pass(rnd, src, pieces, x_sems, c_sems):
        copies = []
        for by in (0, 1, 3, 2):
            slot = core * XCHIPS + (x + XCHIPS - by) % XCHIPS
            if by:
                remote(
                    src, pieces.at[rnd, slot], x_sems[0].at[rnd, by - 1], x_sems[1].at[rnd, by - 1], x_peer(by)
                ).wait_recv()
            copies.append(
                go(
                    pieces.at[rnd, slot] if by else src, pieces.at[rnd, slot],
                    c_sems[0].at[rnd, by], c_sems[1].at[rnd, by], sibling,
                )
            )
        return copies

    def coupling_of(pieces, tile):
        gram_c = jnp.concatenate(
            [jnp.concatenate([pieces[i, :PIECE, :], pieces[i, PIECE:, :]], axis=1) for i in range(PIECES)], axis=0
        )
        inverse = 1.0 / jnp.sqrt(tile + eps_value)
        inv_top = jnp.concatenate([inverse[0:1, :], inverse[1:2, :]], axis=1)
        inv_side = jnp.concatenate([inverse[2:3, :], inverse[3:4, :]], axis=1)
        inv_rows = jnp.sum(jnp.where(on_diagonal, inv_top, 0.0), axis=1, keepdims=True)
        normed = gram_c * inv_rows * inv_side
        total = jnp.sum(jnp.sum(normed * normed, axis=0, keepdims=True), axis=1, keepdims=True)
        return normed * (1.0 / (1.0 + jnp.sqrt(total)))

    unit = jnp.where(on_diagonal, 1.0, 0.0)

    def second_columns(coupling, high_ref, low_ref):
        corner = halves(polar_part(coupling.T, unit))
        turn = product(halves(coupling), corner)
        high_ref[BLK:, :], low_ref[BLK:, :] = corner
        high_ref[:BLK, :], low_ref[:BLK, :] = halves(turn)
        return turn

    for rnd in range(ROUNDS):
        last = rnd == ROUNDS - 1
        order = plan_ref[rnd : rnd + 1, :]
        hot[...] = jnp.where(
            lax.broadcasted_iota(jnp.int32, (WIDTH, WIDTH), 0) == order, 1.0, 0.0
        ).astype(bf16)

        squares = jnp.zeros((1, WIDTH), f32)
        cross = jnp.zeros((BLK, BLK), f32)
        for spot, span in enumerate(FIRST + late):
            if rnd == 0:
                high, low = halves(factor_ref[span, :])
            elif span.start < EARLY:
                high, low = halves(mid[span, :])
            else:
                chunk = spot - len(FIRST)
                there = slice(span.start - EARLY, span.stop - EARLY)
                remote(
                    ship.at[rnd - 1, there, :], land.at[there, :],
                    s_send.at[rnd - 1, chunk], s_recv.at[rnd - 1, chunk], after,
                ).wait_recv()
                sh, sl = halves(land[there, :])
                high = jnp.concatenate([fh[there, :], sh], axis=1)
                low = jnp.concatenate([fl[there, :], sl], axis=1)
            moved_h, moved_l = reorder(high, low)
            wh[span, :] = moved_h.astype(bf16)
            wl[span, :] = moved_l.astype(bf16)
            moved = moved_h + moved_l
            squares += jnp.sum(moved * moved, axis=0, keepdims=True)
            if span.stop % 256 == 0 or (rnd and span.start >= 384):
                begin = span.start if rnd and span.start >= 384 else span.stop - 256
                if rnd and span.stop == 448:
                    begin = 256
                both = slice(begin, span.stop)
                cross += product(
                    (wh[both, :BLK], wl[both, :BLK]), (wh[both, BLK:], wl[both, BLK:]), ((0,), (0,))
                )

        tile = jnp.concatenate(
            [squares[:, i * LANES : (i + 1) * LANES] for i in range(4)] + [jnp.zeros((4, LANES), f32)], axis=0
        )
        for piece in range(PIECES):
            for side in range(2):
                part[rnd, piece, side * PIECE : (side + 1) * PIECE, :] = cross[
                    piece * PIECE : (piece + 1) * PIECE, side * LANES : (side + 1) * LANES
                ]
            part[rnd, piece, TALL:, :] = tile

        if rnd == 0:
            pass_on(7, near_in, 0)
        go(
            part.at[rnd, pl.ds((1 - core) * XCHIPS, XCHIPS)], from_core.at[rnd],
            core_send.at[rnd], core_recv.at[rnd], sibling,
        ).wait_recv()
        for other in range(XCHIPS):
            half_sum[rnd, other] = part[rnd, core * XCHIPS + other] + from_core[rnd, other]

        spread = [
            go(
                half_sum.at[rnd, (x + by) % XCHIPS], from_x.at[rnd, by - 1],
                x_send.at[rnd, by - 1], x_recv.at[rnd, by - 1], x_peer(by),
            )
            for by in (2, 1, 3)
        ]
        for copy in spread:
            copy.wait_recv()
        own_sum[rnd] = (half_sum[rnd, x] + from_x[rnd, 0]) + (from_x[rnd, 1] + from_x[rnd, 2])

        if rnd == 0:
            pass_on(4, far_in, 1)
        swap = go(own_sum.at[rnd], from_z.at[rnd], z_send.at[rnd], z_recv.at[rnd], across)
        raw_src = mid if rnd else factor_ref
        early = [
            functools.partial(
                go, raw_src.at[span, :], raw.at[rnd, span, :], r_send.at[rnd, chunk], r_recv.at[rnd, chunk], after
            )
            for chunk, span in enumerate(FIRST)
        ]
        arriving = [start() for start in early[:AHEAD]]
        swap.wait_recv()
        sum_c[rnd] = own_sum[rnd] + from_z[rnd]
        grid_c[rnd, mine] = sum_c[rnd, :TALL, :]
        own = sum_c.at[rnd, pl.ds(0, TALL)]
        gather_start(rnd, own, grid_c, gx_send, gx_recv)
        hop = go(sum_c.at[rnd], from_before.at[rnd], b_send.at[rnd], b_recv.at[rnd], after)
        arriving += [start() for start in early[AHEAD:]]
        passed = gather_pass(rnd, own, grid_c, (gx_send, gx_recv), (gc_send, gc_recv))
        hop.wait_recv()
        its = from_before.at[rnd, pl.ds(0, TALL)]
        gather_start(rnd, its, grid_b, bx_send, bx_recv)
        for copy in passed:
            copy.wait_recv()

        coupling = coupling_of(grid_c.at[rnd], sum_c[rnd, TALL:, :])
        turn = second_columns(coupling, xh.at[:, BLK:], xl.at[:, BLK:])
        for chunk, span in enumerate(late):
            there = slice(span.start - EARLY, span.stop - EARLY)
            ship[rnd, there, :] = product((wh[span, :], wl[span, :]), (xh[:, BLK:], xl[:, BLK:]))
            go(
                ship.at[rnd, there, :], out_ref.at[span, pl.ds(BLK, BLK)] if last else land.at[there, :],
                s_send.at[rnd, chunk], s_recv.at[rnd, chunk], after,
            )
        shipped = started[-len(late):]

        grid_b[rnd, mine] = from_before[rnd, :TALL, :]
        passed = gather_pass(rnd, its, grid_b, (bx_send, bx_recv), (bc_send, bc_recv))
        xh[:BLK, :BLK], xl[:BLK, :BLK] = halves(polar_part(coupling, unit))
        xh[BLK:, :BLK], xl[BLK:, :BLK] = halves(-turn.T)
        for span in FIRST + late:
            kept = product((wh[span, :], wl[span, :]), (xh[:, :BLK], xl[:, :BLK]))
            if last:
                out_ref[span, :BLK] = kept
            elif span.start < EARLY:
                mid[span, :BLK] = kept
            else:
                there = slice(span.start - EARLY, span.stop - EARLY)
                fh[there, :], fl[there, :] = halves(kept)
        for copy in passed:
            copy.wait_recv()
        second_columns(coupling_of(grid_b.at[rnd], from_before[rnd, TALL:, :]), uh, ul)
        for copy, span in zip(arriving, FIRST):
            copy.wait_recv()
            moved_h, moved_l = reorder(*halves(raw[rnd, span, :]))
            made = product((moved_h.astype(bf16), moved_l.astype(bf16)), (uh[...], ul[...]))
            if last:
                out_ref[span, BLK:] = made
            else:
                mid[span, BLK:] = made

    for copy in shipped:
        copy.wait_recv()
    for copy in started:
        copy.wait_send()


def shards(factor, plan):
    rows = factor.shape[0]
    rest = rows - EARLY
    chunks = len(spans(EARLY, rows, STEP))
    dma = pltpu.SemaphoreType.DMA

    def both(*shape):
        return [dma(shape), dma(shape)]

    return pl.pallas_call(
        kernel,
        out_shape=jax.ShapeDtypeStruct((rows, WIDTH), f32),
        in_specs=[pl.BlockSpec(memory_space=pltpu.VMEM)] * 2,
        out_specs=pl.BlockSpec(memory_space=pltpu.VMEM),
        scratch_shapes=[
            pltpu.VMEM((WIDTH, WIDTH), bf16),
            pltpu.VMEM((rows, WIDTH), bf16),
            pltpu.VMEM((rows, WIDTH), bf16),
            pltpu.VMEM((rest, BLK), bf16),
            pltpu.VMEM((rest, BLK), bf16),
            pltpu.VMEM((WIDTH, WIDTH), bf16),
            pltpu.VMEM((WIDTH, WIDTH), bf16),
            pltpu.VMEM((ROUNDS, PIECES, PACKED, LANES), f32),
            pltpu.VMEM((ROUNDS, XCHIPS, PACKED, LANES), f32),
            pltpu.VMEM((ROUNDS, XCHIPS, PACKED, LANES), f32),
            pltpu.VMEM((ROUNDS, XCHIPS - 1, PACKED, LANES), f32),
            pltpu.VMEM((ROUNDS, PACKED, LANES), f32),
            pltpu.VMEM((ROUNDS, PACKED, LANES), f32),
            pltpu.VMEM((ROUNDS, PACKED, LANES), f32),
            pltpu.VMEM((ROUNDS, PIECES, TALL, LANES), f32),
            pltpu.VMEM((ROUNDS, rest, BLK), f32),
            pltpu.VMEM((rest, BLK), f32),
            pltpu.VMEM((EARLY, WIDTH), f32),
            pltpu.VMEM((ROUNDS, EARLY, WIDTH), f32),
            pltpu.VMEM((WIDTH, BLK), bf16),
            pltpu.VMEM((WIDTH, BLK), bf16),
            pltpu.VMEM((ROUNDS, PACKED, LANES), f32),
            pltpu.VMEM((ROUNDS, PIECES, TALL, LANES), f32),
            *both(ROUNDS), *both(ROUNDS, 3), *both(ROUNDS), *both(ROUNDS, 3), *both(ROUNDS, 4),
            *both(ROUNDS, chunks), *both(ROUNDS, len(FIRST)), *both(ROUNDS), *both(ROUNDS, 3), *both(ROUNDS, 4),
            pltpu.SemaphoreType.REGULAR, pltpu.SemaphoreType.REGULAR,
        ],
        compiler_params=pltpu.CompilerParams(
            collective_id=0, has_side_effects=True, vmem_limit_bytes=24 << 20
        ),
    )(plan, factor)


def solution(mesh):
    placed = (P("row", "pair"), P())
    return jax.shard_map(
        shards, mesh=mesh, in_specs=placed, out_specs=P("row", "pair"), check_vma=False
    )
```

```python
import functools

import jax
import jax.numpy as jnp
from jax import lax
from jax.experimental import pallas as pl
from jax.experimental.pallas import tpu as pltpu
from jax.sharding import PartitionSpec as P

BLK = 256
ROUNDS = 2
WIDTH = 2 * BLK
LANES = 128
XCHIPS = 4
PIECES = 8
PIECE = BLK // PIECES
TALL = 2 * PIECE
PACKED = TALL + 8
EARLY = 256
STEP = 64
SHIP = 128
AHEAD = 1


def spans(low, high, by):
    return tuple(slice(at, min(at + by, high)) for at in range(low, high, by))


FIRST = spans(0, EARLY, STEP)
MESH = pl.DeviceIdType.MESH

eps_value = 1e-06

f32 = jnp.float32
bf16 = jnp.bfloat16


def dot(left, right, dims=((1,), (0,))):
    return lax.dot_general(left, right, (dims, ((), ())), preferred_element_type=f32)


def halves(value):
    high = value.astype(bf16)
    return high, (value - high.astype(f32)).astype(bf16)


def product(left, right, dims=((1,), (0,))):
    (lh, ll), (rh, rl) = left, right
    free = 1 - dims[0][0]
    tall = lh.shape[free]
    both = dot(jnp.concatenate([lh, ll], axis=free), rh, dims)
    return both[:tall] + (both[tall:] + dot(lh, rl, dims))


def polar_part(coupling, unit):
    parts = halves(coupling)
    a = product(parts, parts, ((1,), (1,)))
    ap = halves(a)
    a2 = product(ap, ap)
    e1 = 0.25 * product(halves(a2), ap) - 0.75 * a2
    e1p = halves(e1)
    stacked = product([jnp.concatenate(pair, axis=0) for pair in zip(e1p, ap)], e1p)
    sq = stacked[:BLK]
    e2 = 0.25 * product(halves(sq), e1p) - 0.75 * sq
    off = 0.25 * stacked[BLK:] - 0.5 * (a + e1)
    return unit + (off - 0.5 * (e2 + product(halves(off), halves(e2))))


def kernel(
    plan_ref, factor_ref, out_ref,
    hot, wh, wl, fh, fl, xh, xl, part, from_core, half_sum, from_x, own_sum, from_z, sum_c, grid_c, ship, land,
    mid, raw, vh, vl, uh, ul, from_before, grid_b,
    core_send, core_recv, x_send, x_recv, z_send, z_recv, gx_send, gx_recv, gc_send, gc_recv, s_send, s_recv,
    r_send, r_recv, b_send, b_recv, bx_send, bx_recv, bc_send, bc_recv, near_in, far_in,
):
    pairs = lax.axis_size("pair")
    p, r = lax.axis_index("pair"), lax.axis_index("row")
    core, x, zh = r % 2, (r // 2) % XCHIPS, r // (2 * XCHIPS)
    sibling = (p, r + 1 - 2 * core)
    across = (p, (r + 2 * XCHIPS) % (4 * XCHIPS))
    after, before = ((p + 1) % pairs, r), ((p + pairs - 1) % pairs, r)
    mine = core * XCHIPS + x

    def x_peer(by):
        return (p, zh * (2 * XCHIPS) + ((x + by) % XCHIPS) * 2 + core)

    barrier = pltpu.get_barrier_semaphore()

    def enter(pair, row):
        pl.semaphore_signal(barrier, inc=1, device_id=(pair, row), device_id_type=MESH)

    for by in (1, 2, 3):
        enter(p, x_peer(by)[1] - core)
    enter(across[0], across[1] - core + 1)
    enter(before[0], before[1] - core + 1)

    @pl.when(core == 1)
    def _():
        enter(p, r - 1)

    def pass_on(count, told, teller):
        @pl.when(core == teller)
        def _():
            pl.semaphore_wait(barrier, count)
            pl.semaphore_signal(told, inc=1, device_id=sibling, device_id_type=MESH)

        @pl.when(core != teller)
        def _():
            pl.semaphore_wait(told, 1)

    row_ids = lax.broadcasted_iota(jnp.int32, (BLK, BLK), 0)
    col_ids = lax.broadcasted_iota(jnp.int32, (BLK, BLK), 1)
    on_diagonal = row_ids == col_ids
    rows = out_ref.shape[0]
    whole = slice(0, EARLY)
    late = spans(EARLY, rows, SHIP)

    def remote(src, dst, send, recv, to):
        return pltpu.make_async_remote_copy(
            src_ref=src, dst_ref=dst, send_sem=send, recv_sem=recv, device_id=to, device_id_type=MESH
        )

    started = []

    def go(src, dst, send, recv, to):
        copy = remote(src, dst, send, recv, to)
        copy.start()
        started.append(copy)
        return copy

    def reorder(high, low):
        both = dot(jnp.concatenate([high, low], axis=0), hot[...])
        return both[: high.shape[0]], both[high.shape[0] :]

    def gather_start(rnd, src, pieces, sends, recvs):
        for by in (2, 1, 3):
            go(src, pieces.at[rnd, mine], sends.at[rnd, by - 1], recvs.at[rnd, by - 1], x_peer(by))

    def gather_pass(rnd, src, pieces, x_sems, c_sems):
        copies = []
        for by in (0, 1, 3, 2):
            slot = core * XCHIPS + (x + XCHIPS - by) % XCHIPS
            if by:
                remote(
                    src, pieces.at[rnd, slot], x_sems[0].at[rnd, by - 1], x_sems[1].at[rnd, by - 1], x_peer(by)
                ).wait_recv()
            copies.append(
                go(
                    pieces.at[rnd, slot] if by else src, pieces.at[rnd, slot],
                    c_sems[0].at[rnd, by], c_sems[1].at[rnd, by], sibling,
                )
            )
        return copies

    def coupling_of(pieces, tile):
        gram_c = jnp.concatenate(
            [jnp.concatenate([pieces[i, :PIECE, :], pieces[i, PIECE:, :]], axis=1) for i in range(PIECES)], axis=0
        )
        inverse = 1.0 / jnp.sqrt(tile + eps_value)
        inv_top = jnp.concatenate([inverse[0:1, :], inverse[1:2, :]], axis=1)
        inv_side = jnp.concatenate([inverse[2:3, :], inverse[3:4, :]], axis=1)
        inv_rows = jnp.sum(jnp.where(on_diagonal, inv_top, 0.0), axis=1, keepdims=True)
        normed = gram_c * inv_rows * inv_side
        total = jnp.sum(jnp.sum(normed * normed, axis=0, keepdims=True), axis=1, keepdims=True)
        return normed * (1.0 / (1.0 + jnp.sqrt(total)))

    unit = jnp.where(on_diagonal, 1.0, 0.0)

    def second_columns(coupling, high_ref, low_ref):
        corner = halves(polar_part(coupling.T, unit))
        turn = product(halves(coupling), corner)
        high_ref[BLK:, :], low_ref[BLK:, :] = corner
        high_ref[:BLK, :], low_ref[:BLK, :] = halves(turn)
        return turn

    for rnd in range(ROUNDS):
        last = rnd == ROUNDS - 1
        order = plan_ref[rnd : rnd + 1, :]
        hot[...] = jnp.where(
            lax.broadcasted_iota(jnp.int32, (WIDTH, WIDTH), 0) == order, 1.0, 0.0
        ).astype(bf16)

        squares = jnp.zeros((1, WIDTH), f32)
        cross = jnp.zeros((BLK, BLK), f32)
        for spot, span in enumerate((whole, slice(EARLY, rows)) if rnd == 0 else (whole,) + late):
            if rnd == 0:
                high, low = halves(factor_ref[span, :])
            elif spot == 0:
                high, low = halves(mid[...])
            else:
                there = slice(span.start - EARLY, span.stop - EARLY)
                remote(
                    ship.at[rnd - 1, there, :], land.at[there, :],
                    s_send.at[rnd - 1, spot - 1], s_recv.at[rnd - 1, spot - 1], after,
                ).wait_recv()
                sh, sl = halves(land[there, :])
                high = jnp.concatenate([fh[there, :], sh], axis=1)
                low = jnp.concatenate([fl[there, :], sl], axis=1)
            moved_h, moved_l = reorder(high, low)
            wh[span, :] = moved_h.astype(bf16)
            wl[span, :] = moved_l.astype(bf16)
            moved = moved_h + moved_l
            squares += jnp.sum(moved * moved, axis=0, keepdims=True)
            cross += product((wh[span, :BLK], wl[span, :BLK]), (wh[span, BLK:], wl[span, BLK:]), ((0,), (0,)))

        tile = jnp.concatenate(
            [squares[:, i * LANES : (i + 1) * LANES] for i in range(4)] + [jnp.zeros((4, LANES), f32)], axis=0
        )
        for piece in range(PIECES):
            for side in range(2):
                part[rnd, piece, side * PIECE : (side + 1) * PIECE, :] = cross[
                    piece * PIECE : (piece + 1) * PIECE, side * LANES : (side + 1) * LANES
                ]
            part[rnd, piece, TALL:, :] = tile

        if rnd == 0:
            pass_on(7, near_in, 0)
        go(
            part.at[rnd, pl.ds((1 - core) * XCHIPS, XCHIPS)], from_core.at[rnd],
            core_send.at[rnd], core_recv.at[rnd], sibling,
        ).wait_recv()
        for other in range(XCHIPS):
            half_sum[rnd, other] = part[rnd, core * XCHIPS + other] + from_core[rnd, other]

        spread = [
            go(
                half_sum.at[rnd, (x + by) % XCHIPS], from_x.at[rnd, by - 1],
                x_send.at[rnd, by - 1], x_recv.at[rnd, by - 1], x_peer(by),
            )
            for by in (2, 1, 3)
        ]
        for copy in spread:
            copy.wait_recv()
        own_sum[rnd] = (half_sum[rnd, x] + from_x[rnd, 0]) + (from_x[rnd, 1] + from_x[rnd, 2])

        if rnd == 0:
            pass_on(4, far_in, 1)
        swap = go(own_sum.at[rnd], from_z.at[rnd], z_send.at[rnd], z_recv.at[rnd], across)
        raw_src = mid if rnd else factor_ref
        early = [
            functools.partial(
                go, raw_src.at[span, :], raw.at[rnd, span, :], r_send.at[rnd, chunk], r_recv.at[rnd, chunk], after
            )
            for chunk, span in enumerate(FIRST)
        ]
        arriving = [start() for start in early[:AHEAD]]
        swap.wait_recv()
        sum_c[rnd] = own_sum[rnd] + from_z[rnd]
        grid_c[rnd, mine] = sum_c[rnd, :TALL, :]
        own = sum_c.at[rnd, pl.ds(0, TALL)]
        gather_start(rnd, own, grid_c, gx_send, gx_recv)
        hop = go(sum_c.at[rnd], from_before.at[rnd], b_send.at[rnd], b_recv.at[rnd], after)
        arriving += [start() for start in early[AHEAD:]]
        passed = gather_pass(rnd, own, grid_c, (gx_send, gx_recv), (gc_send, gc_recv))
        hop.wait_recv()
        its = from_before.at[rnd, pl.ds(0, TALL)]
        gather_start(rnd, its, grid_b, bx_send, bx_recv)
        for copy in passed:
            copy.wait_recv()

        coupling = coupling_of(grid_c.at[rnd], sum_c[rnd, TALL:, :])
        turn = second_columns(coupling, xh.at[:, BLK:], xl.at[:, BLK:])
        xh[:BLK, :BLK], xl[:BLK, :BLK] = halves(polar_part(coupling, unit))
        xh[BLK:, :BLK], xl[BLK:, :BLK] = halves(-turn.T)
        for chunk, span in enumerate(late):
            there = slice(span.start - EARLY, span.stop - EARLY)
            ship[rnd, there, :] = product((wh[span, :], wl[span, :]), (xh[:, BLK:], xl[:, BLK:]))
            go(
                ship.at[rnd, there, :], out_ref.at[span, pl.ds(BLK, BLK)] if last else land.at[there, :],
                s_send.at[rnd, chunk], s_recv.at[rnd, chunk], after,
            )
        shipped = started[-len(late):]

        grid_b[rnd, mine] = from_before[rnd, :TALL, :]
        passed = gather_pass(rnd, its, grid_b, (bx_send, bx_recv), (bc_send, bc_recv))
        for span in (whole, slice(EARLY, rows)):
            kept = product((wh[span, :], wl[span, :]), (xh[:, :BLK], xl[:, :BLK]))
            if last:
                out_ref[span, :BLK] = kept
            elif span.start < EARLY:
                mid[:, :BLK] = kept
            else:
                fh[...], fl[...] = halves(kept)
        for copy in arriving:
            copy.wait_recv()
        moved_h, moved_l = reorder(*halves(raw[rnd]))
        vh[...] = moved_h.astype(bf16)
        vl[...] = moved_l.astype(bf16)
        for copy in passed:
            copy.wait_recv()
        second_columns(coupling_of(grid_b.at[rnd], from_before[rnd, TALL:, :]), uh, ul)
        made = product((vh[...], vl[...]), (uh[...], ul[...]))
        if last:
            out_ref[whole, BLK:] = made
        else:
            mid[:, BLK:] = made

    for copy in shipped:
        copy.wait_recv()
    for copy in started:
        copy.wait_send()


def shards(factor, plan):
    rows = factor.shape[0]
    rest = rows - EARLY
    chunks = len(spans(EARLY, rows, SHIP))
    dma = pltpu.SemaphoreType.DMA

    def both(*shape):
        return [dma(shape), dma(shape)]

    return pl.pallas_call(
        kernel,
        out_shape=jax.ShapeDtypeStruct((rows, WIDTH), f32),
        in_specs=[pl.BlockSpec(memory_space=pltpu.VMEM)] * 2,
        out_specs=pl.BlockSpec(memory_space=pltpu.VMEM),
        scratch_shapes=[
            pltpu.VMEM((WIDTH, WIDTH), bf16),
            pltpu.VMEM((rows, WIDTH), bf16),
            pltpu.VMEM((rows, WIDTH), bf16),
            pltpu.VMEM((rest, BLK), bf16),
            pltpu.VMEM((rest, BLK), bf16),
            pltpu.VMEM((WIDTH, WIDTH), bf16),
            pltpu.VMEM((WIDTH, WIDTH), bf16),
            pltpu.VMEM((ROUNDS, PIECES, PACKED, LANES), f32),
            pltpu.VMEM((ROUNDS, XCHIPS, PACKED, LANES), f32),
            pltpu.VMEM((ROUNDS, XCHIPS, PACKED, LANES), f32),
            pltpu.VMEM((ROUNDS, XCHIPS - 1, PACKED, LANES), f32),
            pltpu.VMEM((ROUNDS, PACKED, LANES), f32),
            pltpu.VMEM((ROUNDS, PACKED, LANES), f32),
            pltpu.VMEM((ROUNDS, PACKED, LANES), f32),
            pltpu.VMEM((ROUNDS, PIECES, TALL, LANES), f32),
            pltpu.VMEM((ROUNDS, rest, BLK), f32),
            pltpu.VMEM((rest, BLK), f32),
            pltpu.VMEM((EARLY, WIDTH), f32),
            pltpu.VMEM((ROUNDS, EARLY, WIDTH), f32),
            pltpu.VMEM((EARLY, WIDTH), bf16),
            pltpu.VMEM((EARLY, WIDTH), bf16),
            pltpu.VMEM((WIDTH, BLK), bf16),
            pltpu.VMEM((WIDTH, BLK), bf16),
            pltpu.VMEM((ROUNDS, PACKED, LANES), f32),
            pltpu.VMEM((ROUNDS, PIECES, TALL, LANES), f32),
            *both(ROUNDS), *both(ROUNDS, 3), *both(ROUNDS), *both(ROUNDS, 3), *both(ROUNDS, 4),
            *both(ROUNDS, chunks), *both(ROUNDS, len(FIRST)), *both(ROUNDS), *both(ROUNDS, 3), *both(ROUNDS, 4),
            pltpu.SemaphoreType.REGULAR, pltpu.SemaphoreType.REGULAR,
        ],
        compiler_params=pltpu.CompilerParams(
            collective_id=0, has_side_effects=True, vmem_limit_bytes=24 << 20
        ),
    )(plan, factor)


def solution(mesh):
    placed = (P("row", "pair"), P())
    return jax.shard_map(
        shards, mesh=mesh, in_specs=placed, out_specs=P("row", "pair"), check_vma=False
    )
```

```python
import functools

import jax
import jax.numpy as jnp
from jax import lax
from jax.experimental import pallas as pl
from jax.experimental.pallas import tpu as pltpu
from jax.sharding import PartitionSpec as P

BLK = 256
ROUNDS = 2
WIDTH = 2 * BLK
LANES = 128
XCHIPS = 4
PIECES = 8
PIECE = BLK // PIECES
TALL = 2 * PIECE
PACKED = TALL + 8
EARLY = 192
STEP = 64
SHIP = 128
AHEAD = 1


def spans(low, high, by):
    return tuple(slice(at, min(at + by, high)) for at in range(low, high, by))


FIRST = spans(0, EARLY, STEP)
MESH = pl.DeviceIdType.MESH

eps_value = 1e-06

f32 = jnp.float32
bf16 = jnp.bfloat16


def dot(left, right, dims=((1,), (0,))):
    return lax.dot_general(left, right, (dims, ((), ())), preferred_element_type=f32)


def halves(value):
    high = value.astype(bf16)
    return high, (value - high.astype(f32)).astype(bf16)


def product(left, right, dims=((1,), (0,))):
    (lh, ll), (rh, rl) = left, right
    free = 1 - dims[0][0]
    tall = lh.shape[free]
    both = dot(jnp.concatenate([lh, ll], axis=free), rh, dims)
    return both[:tall] + (both[tall:] + dot(lh, rl, dims))


def polar_factor(b, bp, unit):
    d1 = 0.25 * product(bp, bp) - 0.75 * b
    d1p = halves(d1)
    e1 = product(d1p, bp)
    e1p = halves(e1)
    psi = 0.25 * e1 - 0.5 * (d1 + unit)
    t = product(d1p, e1p)
    step = product(bp, halves(psi))
    u = 0.25 * product(halves(t), e1p) - 0.75 * t
    return psi - 0.5 * (u + product(halves(step), halves(u)))


def kernel(
    plan_ref, factor_ref, out_ref,
    hot, wh, wl, fh, fl, xh, xl, part, from_core, half_sum, from_x, own_sum, from_z, sum_c, grid_c, ship, land,
    mid, raw, vh, vl, uh, ul, from_before, grid_b,
    core_send, core_recv, x_send, x_recv, z_send, z_recv, gx_send, gx_recv, gc_send, gc_recv, s_send, s_recv,
    r_send, r_recv, b_send, b_recv, bx_send, bx_recv, bc_send, bc_recv, near_in, far_in,
):
    pairs = lax.axis_size("pair")
    p, r = lax.axis_index("pair"), lax.axis_index("row")
    core, x, zh = r % 2, (r // 2) % XCHIPS, r // (2 * XCHIPS)
    sibling = (p, r + 1 - 2 * core)
    across = (p, (r + 2 * XCHIPS) % (4 * XCHIPS))
    after, before = ((p + 1) % pairs, r), ((p + pairs - 1) % pairs, r)
    mine = core * XCHIPS + x

    def x_peer(by):
        return (p, zh * (2 * XCHIPS) + ((x + by) % XCHIPS) * 2 + core)

    barrier = pltpu.get_barrier_semaphore()

    def enter(pair, row):
        pl.semaphore_signal(barrier, inc=1, device_id=(pair, row), device_id_type=MESH)

    for by in (1, 2, 3):
        enter(p, x_peer(by)[1] - core)
    enter(across[0], across[1] - core + 1)
    enter(before[0], before[1] - core + 1)

    @pl.when(core == 1)
    def _():
        enter(p, r - 1)

    def pass_on(count, told, teller):
        @pl.when(core == teller)
        def _():
            pl.semaphore_wait(barrier, count)
            pl.semaphore_signal(told, inc=1, device_id=sibling, device_id_type=MESH)

        @pl.when(core != teller)
        def _():
            pl.semaphore_wait(told, 1)

    row_ids = lax.broadcasted_iota(jnp.int32, (BLK, BLK), 0)
    col_ids = lax.broadcasted_iota(jnp.int32, (BLK, BLK), 1)
    on_diagonal = row_ids == col_ids
    rows = out_ref.shape[0]
    whole = slice(0, EARLY)
    late = spans(EARLY, rows, SHIP)

    def remote(src, dst, send, recv, to):
        return pltpu.make_async_remote_copy(
            src_ref=src, dst_ref=dst, send_sem=send, recv_sem=recv, device_id=to, device_id_type=MESH
        )

    started = []

    def go(src, dst, send, recv, to):
        copy = remote(src, dst, send, recv, to)
        copy.start()
        started.append(copy)
        return copy

    def reorder(high, low):
        both = dot(jnp.concatenate([high, low], axis=0), hot[...])
        return both[: high.shape[0]], both[high.shape[0] :]

    def gather_start(rnd, src, pieces, sends, recvs):
        for by in (2, 1, 3):
            go(src, pieces.at[rnd, mine], sends.at[rnd, by - 1], recvs.at[rnd, by - 1], x_peer(by))

    def gather_pass(rnd, src, pieces, x_sems, c_sems):
        copies = []
        for by in (0, 1, 3, 2):
            slot = core * XCHIPS + (x + XCHIPS - by) % XCHIPS
            if by:
                remote(
                    src, pieces.at[rnd, slot], x_sems[0].at[rnd, by - 1], x_sems[1].at[rnd, by - 1], x_peer(by)
                ).wait_recv()
            copies.append(
                go(
                    pieces.at[rnd, slot] if by else src, pieces.at[rnd, slot],
                    c_sems[0].at[rnd, by], c_sems[1].at[rnd, by], sibling,
                )
            )
        return copies

    def coupling_of(pieces, tile):
        gram_c = jnp.concatenate(
            [jnp.concatenate([pieces[i, :PIECE, :], pieces[i, PIECE:, :]], axis=1) for i in range(PIECES)], axis=0
        )
        inverse = 1.0 / jnp.sqrt(tile + eps_value)
        inv_top = jnp.concatenate([inverse[0:1, :], inverse[1:2, :]], axis=1)
        inv_side = jnp.concatenate([inverse[2:3, :], inverse[3:4, :]], axis=1)
        inv_rows = jnp.sum(jnp.where(on_diagonal, inv_top, 0.0), axis=1, keepdims=True)
        normed = gram_c * inv_rows * inv_side
        total = jnp.sum(jnp.sum(normed * normed, axis=0, keepdims=True), axis=1, keepdims=True)
        return normed * (1.0 / (1.0 + jnp.sqrt(total)))

    unit = jnp.where(on_diagonal, 1.0, 0.0)

    def columns_of(coupling, cp):
        tp = halves(coupling.T)
        b = product(tp, tp, ((1,), (1,)))
        bp = halves(b)
        phi = halves(polar_factor(b, bp, unit))
        corner = halves(unit + product(bp, phi))
        return product(cp, corner), corner, phi, tp

    def turned(rnd, chunk, there):
        remote(
            ship.at[rnd, there, :], land.at[rnd, there, :], s_send.at[rnd, chunk], s_recv.at[rnd, chunk], after
        ).wait_recv()
        return product(halves(land[rnd, there, :]), (uh[BLK:, :], ul[BLK:, :]))

    for rnd in range(ROUNDS):
        last = rnd == ROUNDS - 1
        order = plan_ref[rnd : rnd + 1, :]
        hot[...] = jnp.where(
            lax.broadcasted_iota(jnp.int32, (WIDTH, WIDTH), 0) == order, 1.0, 0.0
        ).astype(bf16)

        squares = jnp.zeros((1, WIDTH), f32)
        cross = jnp.zeros((BLK, BLK), f32)
        for spot, span in enumerate((whole, slice(EARLY, rows)) if rnd == 0 else (whole,) + late):
            if rnd == 0:
                high, low = halves(factor_ref[span, :])
            elif spot == 0:
                high, low = halves(mid[...])
            else:
                there = slice(span.start - EARLY, span.stop - EARLY)
                sh, sl = halves(turned(rnd - 1, spot - 1, there))
                high = jnp.concatenate([fh[there, :], sh], axis=1)
                low = jnp.concatenate([fl[there, :], sl], axis=1)
            moved_h, moved_l = reorder(high, low)
            wh[span, :] = moved_h.astype(bf16)
            wl[span, :] = moved_l.astype(bf16)
            moved = moved_h + moved_l
            squares += jnp.sum(moved * moved, axis=0, keepdims=True)
            cross += product((wh[span, :BLK], wl[span, :BLK]), (wh[span, BLK:], wl[span, BLK:]), ((0,), (0,)))

        tile = jnp.concatenate(
            [squares[:, i * LANES : (i + 1) * LANES] for i in range(4)] + [jnp.zeros((4, LANES), f32)], axis=0
        )
        for piece in range(PIECES):
            for side in range(2):
                part[rnd, piece, side * PIECE : (side + 1) * PIECE, :] = cross[
                    piece * PIECE : (piece + 1) * PIECE, side * LANES : (side + 1) * LANES
                ]
            part[rnd, piece, TALL:, :] = tile

        if rnd == 0:
            pass_on(7, near_in, 0)
        go(
            part.at[rnd, pl.ds((1 - core) * XCHIPS, XCHIPS)], from_core.at[rnd],
            core_send.at[rnd], core_recv.at[rnd], sibling,
        ).wait_recv()
        for other in range(XCHIPS):
            half_sum[rnd, other] = part[rnd, core * XCHIPS + other] + from_core[rnd, other]

        spread = [
            go(
                half_sum.at[rnd, (x + by) % XCHIPS], from_x.at[rnd, by - 1],
                x_send.at[rnd, by - 1], x_recv.at[rnd, by - 1], x_peer(by),
            )
            for by in (2, 1, 3)
        ]
        for copy in spread:
            copy.wait_recv()
        own_sum[rnd] = (half_sum[rnd, x] + from_x[rnd, 0]) + (from_x[rnd, 1] + from_x[rnd, 2])

        if rnd == 0:
            pass_on(4, far_in, 1)
        swap = go(own_sum.at[rnd], from_z.at[rnd], z_send.at[rnd], z_recv.at[rnd], across)
        raw_src = mid if rnd else factor_ref
        early = [
            functools.partial(
                go, raw_src.at[span, :], raw.at[rnd, span, :], r_send.at[rnd, chunk], r_recv.at[rnd, chunk], after
            )
            for chunk, span in enumerate(FIRST)
        ]
        arriving = [start() for start in early[:AHEAD]]
        swap.wait_recv()
        sum_c[rnd] = own_sum[rnd] + from_z[rnd]
        grid_c[rnd, mine] = sum_c[rnd, :TALL, :]
        own = sum_c.at[rnd, pl.ds(0, TALL)]
        gather_start(rnd, own, grid_c, gx_send, gx_recv)
        hop = go(sum_c.at[rnd], from_before.at[rnd], b_send.at[rnd], b_recv.at[rnd], after)
        arriving += [start() for start in early[AHEAD:]]
        passed = gather_pass(rnd, own, grid_c, (gx_send, gx_recv), (gc_send, gc_recv))
        hop.wait_recv()
        its = from_before.at[rnd, pl.ds(0, TALL)]
        gather_start(rnd, its, grid_b, bx_send, bx_recv)
        for copy in passed:
            copy.wait_recv()

        coupling = coupling_of(grid_c.at[rnd], sum_c[rnd, TALL:, :])
        cp = halves(coupling)
        for chunk, span in enumerate(late):
            there = slice(span.start - EARLY, span.stop - EARLY)
            second = wh[span, BLK:].astype(f32) + wl[span, BLK:].astype(f32)
            ship[rnd, there, :] = second + product((wh[span, :BLK], wl[span, :BLK]), cp)
            go(
                ship.at[rnd, there, :], land.at[rnd, there, :], s_send.at[rnd, chunk], s_recv.at[rnd, chunk], after
            )
        turn, corner, phi, tp = columns_of(coupling, cp)
        xh[BLK:, :], xl[BLK:, :] = halves(-turn.T)
        xh[:BLK, :], xl[:BLK, :] = halves(unit + product(halves(product(cp, phi)), tp))

        grid_b[rnd, mine] = from_before[rnd, :TALL, :]
        passed = gather_pass(rnd, its, grid_b, (bx_send, bx_recv), (bc_send, bc_recv))
        for span in (whole, slice(EARLY, rows)):
            kept = product((wh[span, :], wl[span, :]), (xh[...], xl[...]))
            if last:
                out_ref[span, :BLK] = kept
            elif span.start < EARLY:
                mid[:, :BLK] = kept
            else:
                fh[...], fl[...] = halves(kept)
        for copy in arriving:
            copy.wait_recv()
        moved_h, moved_l = reorder(*halves(raw[rnd]))
        vh[...] = moved_h.astype(bf16)
        vl[...] = moved_l.astype(bf16)
        for copy in passed:
            copy.wait_recv()
        its_coupling = coupling_of(grid_b.at[rnd], from_before[rnd, TALL:, :])
        its_turn, corner, _, _ = columns_of(its_coupling, halves(its_coupling))
        uh[BLK:, :], ul[BLK:, :] = corner
        uh[:BLK, :], ul[:BLK, :] = halves(its_turn)
        made = product((vh[...], vl[...]), (uh[...], ul[...]))
        if last:
            out_ref[whole, BLK:] = made
        else:
            mid[:, BLK:] = made

    for chunk, span in enumerate(late):
        out_ref[span, BLK:] = turned(ROUNDS - 1, chunk, slice(span.start - EARLY, span.stop - EARLY))
    for copy in started:
        copy.wait_send()


def shards(factor, plan):
    rows = factor.shape[0]
    rest = rows - EARLY
    chunks = len(spans(EARLY, rows, SHIP))
    dma = pltpu.SemaphoreType.DMA

    def both(*shape):
        return [dma(shape), dma(shape)]

    return pl.pallas_call(
        kernel,
        out_shape=jax.ShapeDtypeStruct((rows, WIDTH), f32),
        in_specs=[pl.BlockSpec(memory_space=pltpu.VMEM)] * 2,
        out_specs=pl.BlockSpec(memory_space=pltpu.VMEM),
        scratch_shapes=[
            pltpu.VMEM((WIDTH, WIDTH), bf16),
            pltpu.VMEM((rows, WIDTH), bf16),
            pltpu.VMEM((rows, WIDTH), bf16),
            pltpu.VMEM((rest, BLK), bf16),
            pltpu.VMEM((rest, BLK), bf16),
            pltpu.VMEM((WIDTH, BLK), bf16),
            pltpu.VMEM((WIDTH, BLK), bf16),
            pltpu.VMEM((ROUNDS, PIECES, PACKED, LANES), f32),
            pltpu.VMEM((ROUNDS, XCHIPS, PACKED, LANES), f32),
            pltpu.VMEM((ROUNDS, XCHIPS, PACKED, LANES), f32),
            pltpu.VMEM((ROUNDS, XCHIPS - 1, PACKED, LANES), f32),
            pltpu.VMEM((ROUNDS, PACKED, LANES), f32),
            pltpu.VMEM((ROUNDS, PACKED, LANES), f32),
            pltpu.VMEM((ROUNDS, PACKED, LANES), f32),
            pltpu.VMEM((ROUNDS, PIECES, TALL, LANES), f32),
            pltpu.VMEM((ROUNDS, rest, BLK), f32),
            pltpu.VMEM((ROUNDS, rest, BLK), f32),
            pltpu.VMEM((EARLY, WIDTH), f32),
            pltpu.VMEM((ROUNDS, EARLY, WIDTH), f32),
            pltpu.VMEM((EARLY, WIDTH), bf16),
            pltpu.VMEM((EARLY, WIDTH), bf16),
            pltpu.VMEM((WIDTH, BLK), bf16),
            pltpu.VMEM((WIDTH, BLK), bf16),
            pltpu.VMEM((ROUNDS, PACKED, LANES), f32),
            pltpu.VMEM((ROUNDS, PIECES, TALL, LANES), f32),
            *both(ROUNDS), *both(ROUNDS, 3), *both(ROUNDS), *both(ROUNDS, 3), *both(ROUNDS, 4),
            *both(ROUNDS, chunks), *both(ROUNDS, len(FIRST)), *both(ROUNDS), *both(ROUNDS, 3), *both(ROUNDS, 4),
            pltpu.SemaphoreType.REGULAR, pltpu.SemaphoreType.REGULAR,
        ],
        compiler_params=pltpu.CompilerParams(
            collective_id=0, has_side_effects=True, vmem_limit_bytes=24 << 20
        ),
    )(plan, factor)


def solution(mesh):
    placed = (P("row", "pair"), P())
    return jax.shard_map(
        shards, mesh=mesh, in_specs=placed, out_specs=P("row", "pair"), check_vma=False
    )
```

```python
import functools

import jax
import jax.numpy as jnp
from jax import lax
from jax.experimental import pallas as pl
from jax.experimental.pallas import tpu as pltpu
from jax.sharding import PartitionSpec as P

BLK = 256
ROUNDS = 2
WIDTH = 2 * BLK
LANES = 128
XCHIPS = 4
PIECES = 8
PIECE = BLK // PIECES
TALL = 2 * PIECE
PACKED = TALL + 8
EARLY = 160
STEP = 80
SHIP = 176
AHEAD = 1


def spans(low, high, by):
    return tuple(slice(at, min(at + by, high)) for at in range(low, high, by))


FIRST = spans(0, EARLY, STEP)
MESH = pl.DeviceIdType.MESH

eps_value = 1e-06

f32 = jnp.float32
bf16 = jnp.bfloat16


def dot(left, right, dims=((1,), (0,))):
    return lax.dot_general(left, right, (dims, ((), ())), preferred_element_type=f32)


def halves(value):
    high = value.astype(bf16)
    return high, (value - high.astype(f32)).astype(bf16)


def product(left, right, dims=((1,), (0,))):
    (lh, ll), (rh, rl) = left, right
    free = 1 - dims[0][0]
    tall = lh.shape[free]
    both = dot(jnp.concatenate([lh, ll], axis=free), rh, dims)
    return both[:tall] + (both[tall:] + dot(lh, rl, dims))


def polar_factor(b, bp, unit):
    d1 = 0.25 * product(bp, bp) - 0.75 * b
    d1p = halves(d1)
    e1 = product(d1p, bp)
    e1p = halves(e1)
    psi = 0.25 * e1 - 0.5 * (d1 + unit)
    t = product(d1p, e1p)
    step = product(bp, halves(psi))
    u = 0.25 * product(halves(t), e1p) - 0.75 * t
    return psi - 0.5 * (u + product(halves(step), halves(u)))


def kernel(
    plan_ref, factor_ref, out_ref,
    hot, wh, wl, fh, fl, xh, xl, part, from_core, half_sum, from_x, own_sum, from_z, sum_c, grid_c, ship, land,
    mid, raw, vh, vl, uh, ul, from_before, grid_b,
    core_send, core_recv, x_send, x_recv, z_send, z_recv, gx_send, gx_recv, gc_send, gc_recv, s_send, s_recv,
    r_send, r_recv, b_send, b_recv, bx_send, bx_recv, bc_send, bc_recv, near_in, far_in,
):
    pairs = lax.axis_size("pair")
    p, r = lax.axis_index("pair"), lax.axis_index("row")
    core, x, zh = r % 2, (r // 2) % XCHIPS, r // (2 * XCHIPS)
    sibling = (p, r + 1 - 2 * core)
    across = (p, (r + 2 * XCHIPS) % (4 * XCHIPS))
    after, before = ((p + 1) % pairs, r), ((p + pairs - 1) % pairs, r)
    mine = core * XCHIPS + x

    def x_peer(by):
        return (p, zh * (2 * XCHIPS) + ((x + by) % XCHIPS) * 2 + core)

    barrier = pltpu.get_barrier_semaphore()

    def enter(pair, row):
        pl.semaphore_signal(barrier, inc=1, device_id=(pair, row), device_id_type=MESH)

    for by in (1, 2, 3):
        enter(p, x_peer(by)[1] - core)
    enter(across[0], across[1] - core + 1)
    enter(before[0], before[1] - core + 1)

    @pl.when(core == 1)
    def _():
        enter(p, r - 1)

    def pass_on(count, told, teller):
        @pl.when(core == teller)
        def _():
            pl.semaphore_wait(barrier, count)
            pl.semaphore_signal(told, inc=1, device_id=sibling, device_id_type=MESH)

        @pl.when(core != teller)
        def _():
            pl.semaphore_wait(told, 1)

    row_ids = lax.broadcasted_iota(jnp.int32, (BLK, BLK), 0)
    col_ids = lax.broadcasted_iota(jnp.int32, (BLK, BLK), 1)
    on_diagonal = row_ids == col_ids
    rows = out_ref.shape[0]
    whole = slice(0, EARLY)
    late = spans(EARLY, rows, SHIP)

    def remote(src, dst, send, recv, to):
        return pltpu.make_async_remote_copy(
            src_ref=src, dst_ref=dst, send_sem=send, recv_sem=recv, device_id=to, device_id_type=MESH
        )

    started = []

    def go(src, dst, send, recv, to):
        copy = remote(src, dst, send, recv, to)
        copy.start()
        started.append(copy)
        return copy

    def reorder(high, low):
        both = dot(jnp.concatenate([high, low], axis=0), hot[...])
        return both[: high.shape[0]], both[high.shape[0] :]

    def gather_start(rnd, src, pieces, sends, recvs):
        for by in (2, 1, 3):
            go(src, pieces.at[rnd, mine], sends.at[rnd, by - 1], recvs.at[rnd, by - 1], x_peer(by))

    def gather_pass(rnd, src, pieces, x_sems, c_sems):
        copies = []
        for by in (0, 1, 3, 2):
            slot = core * XCHIPS + (x + XCHIPS - by) % XCHIPS
            if by:
                remote(
                    src, pieces.at[rnd, slot], x_sems[0].at[rnd, by - 1], x_sems[1].at[rnd, by - 1], x_peer(by)
                ).wait_recv()
            copies.append(
                go(
                    pieces.at[rnd, slot] if by else src, pieces.at[rnd, slot],
                    c_sems[0].at[rnd, by], c_sems[1].at[rnd, by], sibling,
                )
            )
        return copies

    def coupling_of(pieces, tile):
        gram_c = jnp.concatenate(
            [jnp.concatenate([pieces[i, :PIECE, :], pieces[i, PIECE:, :]], axis=1) for i in range(PIECES)], axis=0
        )
        inverse = 1.0 / jnp.sqrt(tile + eps_value)
        inv_top = jnp.concatenate([inverse[0:1, :], inverse[1:2, :]], axis=1)
        inv_side = jnp.concatenate([inverse[2:3, :], inverse[3:4, :]], axis=1)
        inv_rows = jnp.sum(jnp.where(on_diagonal, inv_top, 0.0), axis=1, keepdims=True)
        normed = gram_c * inv_rows * inv_side
        total = jnp.sum(jnp.sum(normed * normed, axis=0, keepdims=True), axis=1, keepdims=True)
        return normed * (1.0 / (1.0 + jnp.sqrt(total)))

    unit = jnp.where(on_diagonal, 1.0, 0.0)

    def columns_of(coupling, cp):
        tp = halves(coupling.T)
        b = product(tp, tp, ((1,), (1,)))
        bp = halves(b)
        phi = halves(polar_factor(b, bp, unit))
        corner = halves(unit + product(bp, phi))
        return product(cp, corner), corner, phi, tp

    def turned(rnd, chunk, there):
        remote(
            ship.at[rnd, there, :], land.at[rnd, there, :], s_send.at[rnd, chunk], s_recv.at[rnd, chunk], after
        ).wait_recv()
        return product(halves(land[rnd, there, :]), (uh[BLK:, :], ul[BLK:, :]))

    for rnd in range(ROUNDS):
        last = rnd == ROUNDS - 1
        order = plan_ref[rnd : rnd + 1, :]
        hot[...] = jnp.where(
            lax.broadcasted_iota(jnp.int32, (WIDTH, WIDTH), 0) == order, 1.0, 0.0
        ).astype(bf16)

        squares = jnp.zeros((1, WIDTH), f32)
        cross = jnp.zeros((BLK, BLK), f32)
        for spot, span in enumerate((whole, slice(EARLY, rows)) if rnd == 0 else (whole,) + late):
            if rnd == 0:
                high, low = halves(factor_ref[span, :])
            elif spot == 0:
                high, low = halves(mid[...])
            else:
                there = slice(span.start - EARLY, span.stop - EARLY)
                sh, sl = halves(turned(rnd - 1, spot - 1, there))
                high = jnp.concatenate([fh[there, :], sh], axis=1)
                low = jnp.concatenate([fl[there, :], sl], axis=1)
            moved_h, moved_l = reorder(high, low)
            wh[span, :] = moved_h.astype(bf16)
            wl[span, :] = moved_l.astype(bf16)
            moved = moved_h + moved_l
            squares += jnp.sum(moved * moved, axis=0, keepdims=True)
            cross += product((wh[span, :BLK], wl[span, :BLK]), (wh[span, BLK:], wl[span, BLK:]), ((0,), (0,)))

        tile = jnp.concatenate(
            [squares[:, i * LANES : (i + 1) * LANES] for i in range(4)] + [jnp.zeros((4, LANES), f32)], axis=0
        )
        for piece in range(PIECES):
            for side in range(2):
                part[rnd, piece, side * PIECE : (side + 1) * PIECE, :] = cross[
                    piece * PIECE : (piece + 1) * PIECE, side * LANES : (side + 1) * LANES
                ]
            part[rnd, piece, TALL:, :] = tile

        if rnd == 0:
            pass_on(7, near_in, 0)
        go(
            part.at[rnd, pl.ds((1 - core) * XCHIPS, XCHIPS)], from_core.at[rnd],
            core_send.at[rnd], core_recv.at[rnd], sibling,
        ).wait_recv()
        for other in range(XCHIPS):
            half_sum[rnd, other] = part[rnd, core * XCHIPS + other] + from_core[rnd, other]

        spread = [
            go(
                half_sum.at[rnd, (x + by) % XCHIPS], from_x.at[rnd, by - 1],
                x_send.at[rnd, by - 1], x_recv.at[rnd, by - 1], x_peer(by),
            )
            for by in (2, 1, 3)
        ]
        for copy in spread:
            copy.wait_recv()
        own_sum[rnd] = (half_sum[rnd, x] + from_x[rnd, 0]) + (from_x[rnd, 1] + from_x[rnd, 2])

        if rnd == 0:
            pass_on(4, far_in, 1)
        swap = go(own_sum.at[rnd], from_z.at[rnd], z_send.at[rnd], z_recv.at[rnd], across)
        raw_src = mid if rnd else factor_ref
        early = [
            functools.partial(
                go, raw_src.at[span, :], raw.at[rnd, span, :], r_send.at[rnd, chunk], r_recv.at[rnd, chunk], after
            )
            for chunk, span in enumerate(FIRST)
        ]
        arriving = [start() for start in early[:AHEAD]]
        swap.wait_recv()
        sum_c[rnd] = own_sum[rnd] + from_z[rnd]
        grid_c[rnd, mine] = sum_c[rnd, :TALL, :]
        own = sum_c.at[rnd, pl.ds(0, TALL)]
        gather_start(rnd, own, grid_c, gx_send, gx_recv)
        hop = go(sum_c.at[rnd], from_before.at[rnd], b_send.at[rnd], b_recv.at[rnd], after)
        arriving += [start() for start in early[AHEAD:]]
        passed = gather_pass(rnd, own, grid_c, (gx_send, gx_recv), (gc_send, gc_recv))
        hop.wait_recv()
        its = from_before.at[rnd, pl.ds(0, TALL)]
        gather_start(rnd, its, grid_b, bx_send, bx_recv)
        for copy in passed:
            copy.wait_recv()

        coupling = coupling_of(grid_c.at[rnd], sum_c[rnd, TALL:, :])
        cp = halves(coupling)
        for chunk, span in enumerate(late):
            there = slice(span.start - EARLY, span.stop - EARLY)
            second = wh[span, BLK:].astype(f32) + wl[span, BLK:].astype(f32)
            ship[rnd, there, :] = second + product((wh[span, :BLK], wl[span, :BLK]), cp)
            go(
                ship.at[rnd, there, :], land.at[rnd, there, :], s_send.at[rnd, chunk], s_recv.at[rnd, chunk], after
            )
        turn, corner, phi, tp = columns_of(coupling, cp)
        xh[BLK:, :], xl[BLK:, :] = halves(-turn.T)
        xh[:BLK, :], xl[:BLK, :] = halves(unit + product(halves(product(cp, phi)), tp))

        grid_b[rnd, mine] = from_before[rnd, :TALL, :]
        passed = gather_pass(rnd, its, grid_b, (bx_send, bx_recv), (bc_send, bc_recv))
        for span in (whole, slice(EARLY, rows)):
            kept = product((wh[span, :], wl[span, :]), (xh[...], xl[...]))
            if last:
                out_ref[span, :BLK] = kept
            elif span.start < EARLY:
                mid[:, :BLK] = kept
            else:
                fh[...], fl[...] = halves(kept)
        for copy in arriving:
            copy.wait_recv()
        moved_h, moved_l = reorder(*halves(raw[rnd]))
        vh[...] = moved_h.astype(bf16)
        vl[...] = moved_l.astype(bf16)
        for copy in passed:
            copy.wait_recv()
        its_coupling = coupling_of(grid_b.at[rnd], from_before[rnd, TALL:, :])
        its_turn, corner, _, _ = columns_of(its_coupling, halves(its_coupling))
        uh[BLK:, :], ul[BLK:, :] = corner
        uh[:BLK, :], ul[:BLK, :] = halves(its_turn)
        made = product((vh[...], vl[...]), (uh[...], ul[...]))
        if last:
            out_ref[whole, BLK:] = made
        else:
            mid[:, BLK:] = made

    for chunk, span in enumerate(late):
        out_ref[span, BLK:] = turned(ROUNDS - 1, chunk, slice(span.start - EARLY, span.stop - EARLY))
    for copy in started:
        copy.wait_send()


def shards(factor, plan):
    rows = factor.shape[0]
    rest = rows - EARLY
    chunks = len(spans(EARLY, rows, SHIP))
    dma = pltpu.SemaphoreType.DMA

    def both(*shape):
        return [dma(shape), dma(shape)]

    return pl.pallas_call(
        kernel,
        out_shape=jax.ShapeDtypeStruct((rows, WIDTH), f32),
        in_specs=[pl.BlockSpec(memory_space=pltpu.VMEM)] * 2,
        out_specs=pl.BlockSpec(memory_space=pltpu.VMEM),
        scratch_shapes=[
            pltpu.VMEM((WIDTH, WIDTH), bf16),
            pltpu.VMEM((rows, WIDTH), bf16),
            pltpu.VMEM((rows, WIDTH), bf16),
            pltpu.VMEM((rest, BLK), bf16),
            pltpu.VMEM((rest, BLK), bf16),
            pltpu.VMEM((WIDTH, BLK), bf16),
            pltpu.VMEM((WIDTH, BLK), bf16),
            pltpu.VMEM((ROUNDS, PIECES, PACKED, LANES), f32),
            pltpu.VMEM((ROUNDS, XCHIPS, PACKED, LANES), f32),
            pltpu.VMEM((ROUNDS, XCHIPS, PACKED, LANES), f32),
            pltpu.VMEM((ROUNDS, XCHIPS - 1, PACKED, LANES), f32),
            pltpu.VMEM((ROUNDS, PACKED, LANES), f32),
            pltpu.VMEM((ROUNDS, PACKED, LANES), f32),
            pltpu.VMEM((ROUNDS, PACKED, LANES), f32),
            pltpu.VMEM((ROUNDS, PIECES, TALL, LANES), f32),
            pltpu.VMEM((ROUNDS, rest, BLK), f32),
            pltpu.VMEM((ROUNDS, rest, BLK), f32),
            pltpu.VMEM((EARLY, WIDTH), f32),
            pltpu.VMEM((ROUNDS, EARLY, WIDTH), f32),
            pltpu.VMEM((EARLY, WIDTH), bf16),
            pltpu.VMEM((EARLY, WIDTH), bf16),
            pltpu.VMEM((WIDTH, BLK), bf16),
            pltpu.VMEM((WIDTH, BLK), bf16),
            pltpu.VMEM((ROUNDS, PACKED, LANES), f32),
            pltpu.VMEM((ROUNDS, PIECES, TALL, LANES), f32),
            *both(ROUNDS), *both(ROUNDS, 3), *both(ROUNDS), *both(ROUNDS, 3), *both(ROUNDS, 4),
            *both(ROUNDS, chunks), *both(ROUNDS, len(FIRST)), *both(ROUNDS), *both(ROUNDS, 3), *both(ROUNDS, 4),
            pltpu.SemaphoreType.REGULAR, pltpu.SemaphoreType.REGULAR,
        ],
        compiler_params=pltpu.CompilerParams(
            collective_id=0, has_side_effects=True, vmem_limit_bytes=24 << 20
        ),
    )(plan, factor)


def solution(mesh):
    placed = (P("row", "pair"), P())
    return jax.shard_map(
        shards, mesh=mesh, in_specs=placed, out_specs=P("row", "pair"), check_vma=False
    )
```

```python
import functools

import jax
import jax.numpy as jnp
from jax import lax
from jax.experimental import pallas as pl
from jax.experimental.pallas import tpu as pltpu
from jax.sharding import PartitionSpec as P

BLK = 256
ROUNDS = 2
WIDTH = 2 * BLK
LANES = 128
XCHIPS = 4
PIECES = 8
PIECE = BLK // PIECES
TALL = 2 * PIECE
PACKED = TALL + 8
EARLY = 160
STEP = 64
SHIP = 176
AHEAD = 1


def spans(low, high, by):
    return tuple(slice(at, min(at + by, high)) for at in range(low, high, by))


FIRST = spans(0, EARLY, STEP)
MESH = pl.DeviceIdType.MESH

eps_value = 1e-06

f32 = jnp.float32
bf16 = jnp.bfloat16


def dot(left, right, dims=((1,), (0,))):
    return lax.dot_general(left, right, (dims, ((), ())), preferred_element_type=f32)


def halves(value):
    high = value.astype(bf16)
    return high, (value - high.astype(f32)).astype(bf16)


def product(left, right, dims=((1,), (0,))):
    (lh, ll), (rh, rl) = left, right
    free = 1 - dims[0][0]
    tall = lh.shape[free]
    both = dot(jnp.concatenate([lh, ll], axis=free), rh, dims)
    return both[:tall] + (both[tall:] + dot(lh, rl, dims))


def polar_factor(b, bp, unit):
    d1 = 0.25 * product(bp, bp) - 0.75 * b
    d1p = halves(d1)
    e1 = product(d1p, bp)
    e1p = halves(e1)
    psi = 0.25 * e1 - 0.5 * (d1 + unit)
    t = product(d1p, e1p)
    step = product(bp, halves(psi))
    u = 0.25 * product(halves(t), e1p) - 0.75 * t
    return psi - 0.5 * (u + product(halves(step), halves(u)))


def kernel(
    plan_ref, factor_ref, out_ref,
    hot, wh, wl, fh, fl, xh, xl, part, from_core, half_sum, from_x, own_sum, from_z, sum_c, grid_c, ship, land,
    mid, raw, vh, vl, uh, ul, from_before, grid_b,
    core_send, core_recv, x_send, x_recv, z_send, z_recv, gx_send, gx_recv, gc_send, gc_recv, s_send, s_recv,
    r_send, r_recv, b_send, b_recv, bx_send, bx_recv, bc_send, bc_recv, near_in, far_in,
):
    pairs = lax.axis_size("pair")
    p, r = lax.axis_index("pair"), lax.axis_index("row")
    core, x, zh = r % 2, (r // 2) % XCHIPS, r // (2 * XCHIPS)
    sibling = (p, r + 1 - 2 * core)
    across = (p, (r + 2 * XCHIPS) % (4 * XCHIPS))
    after, before = ((p + 1) % pairs, r), ((p + pairs - 1) % pairs, r)
    mine = core * XCHIPS + x

    def x_peer(by):
        return (p, zh * (2 * XCHIPS) + ((x + by) % XCHIPS) * 2 + core)

    barrier = pltpu.get_barrier_semaphore()

    def enter(pair, row):
        pl.semaphore_signal(barrier, inc=1, device_id=(pair, row), device_id_type=MESH)

    for by in (1, 2, 3):
        enter(p, x_peer(by)[1] - core)
    enter(across[0], across[1] - core + 1)
    enter(before[0], before[1] - core + 1)

    @pl.when(core == 1)
    def _():
        enter(p, r - 1)

    def pass_on(count, told, teller):
        @pl.when(core == teller)
        def _():
            pl.semaphore_wait(barrier, count)
            pl.semaphore_signal(told, inc=1, device_id=sibling, device_id_type=MESH)

        @pl.when(core != teller)
        def _():
            pl.semaphore_wait(told, 1)

    row_ids = lax.broadcasted_iota(jnp.int32, (BLK, BLK), 0)
    col_ids = lax.broadcasted_iota(jnp.int32, (BLK, BLK), 1)
    on_diagonal = row_ids == col_ids
    rows = out_ref.shape[0]
    whole = slice(0, EARLY)
    late = spans(EARLY, rows, SHIP)

    def remote(src, dst, send, recv, to):
        return pltpu.make_async_remote_copy(
            src_ref=src, dst_ref=dst, send_sem=send, recv_sem=recv, device_id=to, device_id_type=MESH
        )

    started = []

    def go(src, dst, send, recv, to):
        copy = remote(src, dst, send, recv, to)
        copy.start()
        started.append(copy)
        return copy

    def reorder(high, low):
        both = dot(jnp.concatenate([high, low], axis=0), hot[...])
        return both[: high.shape[0]], both[high.shape[0] :]

    def gather_start(rnd, src, pieces, sends, recvs):
        for by in (2, 1, 3):
            go(src, pieces.at[rnd, mine], sends.at[rnd, by - 1], recvs.at[rnd, by - 1], x_peer(by))

    def gather_pass(rnd, src, pieces, x_sems, c_sems):
        copies = []
        for by in (0, 1, 3, 2):
            slot = core * XCHIPS + (x + XCHIPS - by) % XCHIPS
            if by:
                remote(
                    src, pieces.at[rnd, slot], x_sems[0].at[rnd, by - 1], x_sems[1].at[rnd, by - 1], x_peer(by)
                ).wait_recv()
            copies.append(
                go(
                    pieces.at[rnd, slot] if by else src, pieces.at[rnd, slot],
                    c_sems[0].at[rnd, by], c_sems[1].at[rnd, by], sibling,
                )
            )
        return copies

    def coupling_of(pieces, tile):
        gram_c = jnp.concatenate(
            [jnp.concatenate([pieces[i, :PIECE, :], pieces[i, PIECE:, :]], axis=1) for i in range(PIECES)], axis=0
        )
        inverse = 1.0 / jnp.sqrt(tile + eps_value)
        inv_top = jnp.concatenate([inverse[0:1, :], inverse[1:2, :]], axis=1)
        inv_side = jnp.concatenate([inverse[2:3, :], inverse[3:4, :]], axis=1)
        inv_rows = jnp.sum(jnp.where(on_diagonal, inv_top, 0.0), axis=1, keepdims=True)
        normed = gram_c * inv_rows * inv_side
        total = jnp.sum(jnp.sum(normed * normed, axis=0, keepdims=True), axis=1, keepdims=True)
        return normed * (1.0 / (1.0 + jnp.sqrt(total)))

    unit = jnp.where(on_diagonal, 1.0, 0.0)

    def columns_of(coupling, cp):
        tp = halves(coupling.T)
        b = product(tp, tp, ((1,), (1,)))
        bp = halves(b)
        phi = halves(polar_factor(b, bp, unit))
        corner = halves(unit + product(bp, phi))
        return product(cp, corner), corner, phi, tp

    def turned(rnd, chunk, there):
        remote(
            ship.at[rnd, there, :], land.at[rnd, there, :], s_send.at[rnd, chunk], s_recv.at[rnd, chunk], after
        ).wait_recv()
        return product(halves(land[rnd, there, :]), (uh[BLK:, :], ul[BLK:, :]))

    for rnd in range(ROUNDS):
        last = rnd == ROUNDS - 1
        order = plan_ref[rnd : rnd + 1, :]
        hot[...] = jnp.where(
            lax.broadcasted_iota(jnp.int32, (WIDTH, WIDTH), 0) == order, 1.0, 0.0
        ).astype(bf16)

        squares = jnp.zeros((1, WIDTH), f32)
        cross = jnp.zeros((BLK, BLK), f32)
        for spot, span in enumerate((whole, slice(EARLY, rows)) if rnd == 0 else (whole,) + late):
            if rnd == 0:
                high, low = halves(factor_ref[span, :])
            elif spot == 0:
                high, low = halves(mid[...])
            else:
                there = slice(span.start - EARLY, span.stop - EARLY)
                sh, sl = halves(turned(rnd - 1, spot - 1, there))
                high = jnp.concatenate([fh[there, :], sh], axis=1)
                low = jnp.concatenate([fl[there, :], sl], axis=1)
            moved_h, moved_l = reorder(high, low)
            wh[span, :] = moved_h.astype(bf16)
            wl[span, :] = moved_l.astype(bf16)
            moved = moved_h + moved_l
            squares += jnp.sum(moved * moved, axis=0, keepdims=True)
            cross += product((wh[span, :BLK], wl[span, :BLK]), (wh[span, BLK:], wl[span, BLK:]), ((0,), (0,)))

        tile = jnp.concatenate(
            [squares[:, i * LANES : (i + 1) * LANES] for i in range(4)] + [jnp.zeros((4, LANES), f32)], axis=0
        )
        for piece in range(PIECES):
            for side in range(2):
                part[rnd, piece, side * PIECE : (side + 1) * PIECE, :] = cross[
                    piece * PIECE : (piece + 1) * PIECE, side * LANES : (side + 1) * LANES
                ]
            part[rnd, piece, TALL:, :] = tile

        if rnd == 0:
            pass_on(7, near_in, 0)
        go(
            part.at[rnd, pl.ds((1 - core) * XCHIPS, XCHIPS)], from_core.at[rnd],
            core_send.at[rnd], core_recv.at[rnd], sibling,
        ).wait_recv()
        for other in range(XCHIPS):
            half_sum[rnd, other] = part[rnd, core * XCHIPS + other] + from_core[rnd, other]

        spread = [
            go(
                half_sum.at[rnd, (x + by) % XCHIPS], from_x.at[rnd, by - 1],
                x_send.at[rnd, by - 1], x_recv.at[rnd, by - 1], x_peer(by),
            )
            for by in (2, 1, 3)
        ]
        for copy in spread:
            copy.wait_recv()
        own_sum[rnd] = (half_sum[rnd, x] + from_x[rnd, 0]) + (from_x[rnd, 1] + from_x[rnd, 2])

        if rnd == 0:
            pass_on(4, far_in, 1)
        swap = go(own_sum.at[rnd], from_z.at[rnd], z_send.at[rnd], z_recv.at[rnd], across)
        raw_src = mid if rnd else factor_ref
        early = [
            functools.partial(
                go, raw_src.at[span, :], raw.at[rnd, span, :], r_send.at[rnd, chunk], r_recv.at[rnd, chunk], after
            )
            for chunk, span in enumerate(FIRST)
        ]
        arriving = [start() for start in early[:AHEAD]]
        swap.wait_recv()
        sum_c[rnd] = own_sum[rnd] + from_z[rnd]
        grid_c[rnd, mine] = sum_c[rnd, :TALL, :]
        own = sum_c.at[rnd, pl.ds(0, TALL)]
        gather_start(rnd, own, grid_c, gx_send, gx_recv)
        hop = go(sum_c.at[rnd], from_before.at[rnd], b_send.at[rnd], b_recv.at[rnd], after)
        arriving += [start() for start in early[AHEAD:]]
        passed = gather_pass(rnd, own, grid_c, (gx_send, gx_recv), (gc_send, gc_recv))
        hop.wait_recv()
        its = from_before.at[rnd, pl.ds(0, TALL)]
        gather_start(rnd, its, grid_b, bx_send, bx_recv)
        for copy in passed:
            copy.wait_recv()

        coupling = coupling_of(grid_c.at[rnd], sum_c[rnd, TALL:, :])
        cp = halves(coupling)
        for chunk, span in enumerate(late):
            there = slice(span.start - EARLY, span.stop - EARLY)
            second = wh[span, BLK:].astype(f32) + wl[span, BLK:].astype(f32)
            ship[rnd, there, :] = second + product((wh[span, :BLK], wl[span, :BLK]), cp)
            go(
                ship.at[rnd, there, :], land.at[rnd, there, :], s_send.at[rnd, chunk], s_recv.at[rnd, chunk], after
            )
        turn, corner, phi, tp = columns_of(coupling, cp)
        xh[BLK:, :], xl[BLK:, :] = halves(-turn.T)
        xh[:BLK, :], xl[:BLK, :] = halves(unit + product(halves(product(cp, phi)), tp))

        grid_b[rnd, mine] = from_before[rnd, :TALL, :]
        passed = gather_pass(rnd, its, grid_b, (bx_send, bx_recv), (bc_send, bc_recv))
        for span in (whole, slice(EARLY, rows)):
            kept = product((wh[span, :], wl[span, :]), (xh[...], xl[...]))
            if last:
                out_ref[span, :BLK] = kept
            elif span.start < EARLY:
                mid[:, :BLK] = kept
            else:
                fh[...], fl[...] = halves(kept)
        for copy in arriving:
            copy.wait_recv()
        moved_h, moved_l = reorder(*halves(raw[rnd]))
        vh[...] = moved_h.astype(bf16)
        vl[...] = moved_l.astype(bf16)
        for copy in passed:
            copy.wait_recv()
        its_coupling = coupling_of(grid_b.at[rnd], from_before[rnd, TALL:, :])
        its_turn, corner, _, _ = columns_of(its_coupling, halves(its_coupling))
        uh[BLK:, :], ul[BLK:, :] = corner
        uh[:BLK, :], ul[:BLK, :] = halves(its_turn)
        made = product((vh[...], vl[...]), (uh[...], ul[...]))
        if last:
            out_ref[whole, BLK:] = made
        else:
            mid[:, BLK:] = made

    for chunk, span in enumerate(late):
        out_ref[span, BLK:] = turned(ROUNDS - 1, chunk, slice(span.start - EARLY, span.stop - EARLY))
    for copy in started:
        copy.wait_send()


def shards(factor, plan):
    rows = factor.shape[0]
    rest = rows - EARLY
    chunks = len(spans(EARLY, rows, SHIP))
    dma = pltpu.SemaphoreType.DMA

    def both(*shape):
        return [dma(shape), dma(shape)]

    return pl.pallas_call(
        kernel,
        out_shape=jax.ShapeDtypeStruct((rows, WIDTH), f32),
        in_specs=[pl.BlockSpec(memory_space=pltpu.VMEM)] * 2,
        out_specs=pl.BlockSpec(memory_space=pltpu.VMEM),
        scratch_shapes=[
            pltpu.VMEM((WIDTH, WIDTH), bf16),
            pltpu.VMEM((rows, WIDTH), bf16),
            pltpu.VMEM((rows, WIDTH), bf16),
            pltpu.VMEM((rest, BLK), bf16),
            pltpu.VMEM((rest, BLK), bf16),
            pltpu.VMEM((WIDTH, BLK), bf16),
            pltpu.VMEM((WIDTH, BLK), bf16),
            pltpu.VMEM((ROUNDS, PIECES, PACKED, LANES), f32),
            pltpu.VMEM((ROUNDS, XCHIPS, PACKED, LANES), f32),
            pltpu.VMEM((ROUNDS, XCHIPS, PACKED, LANES), f32),
            pltpu.VMEM((ROUNDS, XCHIPS - 1, PACKED, LANES), f32),
            pltpu.VMEM((ROUNDS, PACKED, LANES), f32),
            pltpu.VMEM((ROUNDS, PACKED, LANES), f32),
            pltpu.VMEM((ROUNDS, PACKED, LANES), f32),
            pltpu.VMEM((ROUNDS, PIECES, TALL, LANES), f32),
            pltpu.VMEM((ROUNDS, rest, BLK), f32),
            pltpu.VMEM((ROUNDS, rest, BLK), f32),
            pltpu.VMEM((EARLY, WIDTH), f32),
            pltpu.VMEM((ROUNDS, EARLY, WIDTH), f32),
            pltpu.VMEM((EARLY, WIDTH), bf16),
            pltpu.VMEM((EARLY, WIDTH), bf16),
            pltpu.VMEM((WIDTH, BLK), bf16),
            pltpu.VMEM((WIDTH, BLK), bf16),
            pltpu.VMEM((ROUNDS, PACKED, LANES), f32),
            pltpu.VMEM((ROUNDS, PIECES, TALL, LANES), f32),
            *both(ROUNDS), *both(ROUNDS, 3), *both(ROUNDS), *both(ROUNDS, 3), *both(ROUNDS, 4),
            *both(ROUNDS, chunks), *both(ROUNDS, len(FIRST)), *both(ROUNDS), *both(ROUNDS, 3), *both(ROUNDS, 4),
            pltpu.SemaphoreType.REGULAR, pltpu.SemaphoreType.REGULAR,
        ],
        compiler_params=pltpu.CompilerParams(
            collective_id=0, has_side_effects=True, vmem_limit_bytes=24 << 20
        ),
    )(plan, factor)


def solution(mesh):
    placed = (P("row", "pair"), P())
    return jax.shard_map(
        shards, mesh=mesh, in_specs=placed, out_specs=P("row", "pair"), check_vma=False
    )
```
